256 devices in a mesh: wide: 16 (over y_lo, z), row: 16 (over y_hi, x, core).
Axes of the slice: x: 4, y: 4 (y_hi: 2, y_lo: 2; y = y_hi * 2 + y_lo), z: 8, core: 2. Of those that a mesh axis runs over, the one named last changes fastest.
Arguments:
- hessian: float32 [18432, 18432], P('row', 'wide'), as said below
- weight: bfloat16 [4608, 18432], P('row', 'wide'), may hold values from -6 to 6
- pairs: int32 [2], replicated, may hold values from 0 to 47, as said below
Outputs:
- pruned_hessian: float32 [18432, 18432], P('row', 'wide')
- pruned_weight: bfloat16 [4608, 18432], P('row', 'wide')
The draws below stay inside these ranges and needn't reach their ends.
Inputs may be any that keep to these rules, and one draw needn't show every extreme that they name: Two different head pairs, one of which is the last pair, 47. `hessian`: symmetric positive definite.
All inputs are finite; a program needn't handle non-finite values.
Results may differ from the reference program's by a relative error of at most 0.001.
Values may be sent and summed in bfloat16 or wider, within the bound.
A program may use at most 128 MiB of HBM per device.

```python
import jax
import jax.numpy as jnp
from jax import lax

HEAD = 192
K = 18432
NPAIRS = 48
DOUT = 4608


low_rank = 16


def draw_hessian(key, part):
    key_raw = jax.random.fold_in(key, 0)
    key_diag = jax.random.fold_in(key, 1)
    key_low = jax.random.fold_in(key, 3)
    raw_part = jax.random.uniform(key_raw, (K, K), jnp.float32, -1.0, 1.0) * 3.0 ** 0.5 / K ** 0.5
    symmetric = (raw_part + raw_part.T) * 0.5 ** 0.5
    diagonal = jax.random.uniform(key_diag, (K,), jnp.float32, 2.5, 5.0)
    indices = jnp.arange(K)
    symmetric = jnp.where(indices[:, None] == indices[None, :], diagonal[:, None], symmetric)
    factors = jax.random.randint(key_low, (K, low_rank), -6, 7).astype(jnp.float32) / 32.0
    shared = jnp.dot(factors, factors.T, precision=lax.Precision.HIGHEST)
    symmetric = symmetric + shared
    return symmetric


def draw_pairs(key, part):
    key_other, key_order = jax.random.split(jax.random.fold_in(key, 7))
    other_pair = jax.random.randint(key_other, (), 0, NPAIRS - 1).astype(jnp.int32)
    last_pair = jnp.array(NPAIRS - 1, jnp.int32)
    flip = jax.random.randint(key_order, (), 0, 2).astype(jnp.int32)
    first = jnp.where(flip == 0, other_pair, last_pair)
    second = jnp.where(flip == 0, last_pair, other_pair)
    return jnp.stack([first, second]).astype(jnp.int32)


def shard_levels(key, shape, shards, least, high):
    def one(position, blocks):
        heights = jax.random.uniform(jax.random.fold_in(jax.random.fold_in(key, 6), position), (blocks,), jnp.float32, least / len(shards), high / len(shards))
        return jnp.repeat(jnp.exp(heights), shape[position] // blocks).reshape((-1,) + (1,) * (len(shape) - position - 1))

    level = one(*shards[0])
    for cut in shards[1:]:
        level = level * one(*cut)
    return level


def scatter_about(stream_key, shape, spread, bound, pieces=(), kind=jnp.bfloat16):
    values = spread * jax.random.normal(stream_key, shape, jnp.float32)
    if pieces:
        values = values * shard_levels(stream_key, shape, pieces, -0.22, 0.18)
    return jnp.clip(values, -bound, bound).astype(kind)


def setup_inputs(seed: int = 0) -> dict:
    keys = jax.random.split(jax.random.key(seed), 4)
    return {
        "hessian": draw_hessian(jax.random.fold_in(keys[3], 71), 0),
        "weight": scatter_about(keys[1], (DOUT, K), 1.0, 6.0, ((0, 16), (1, 16))),
        "pairs": draw_pairs(jax.random.fold_in(keys[3], 71), 0),
    }


def prune_pair(matrix, weights, pair_index):
    pair_width = 2 * HEAD
    first_col = (pair_index * pair_width).astype(jnp.int32)
    column_panel = lax.dynamic_slice_in_dim(matrix, first_col, pair_width, 1)
    pivot_block = lax.dynamic_slice_in_dim(column_panel, first_col, pair_width, 0)
    row_panel = lax.dynamic_slice_in_dim(matrix, first_col, pair_width, 0)
    factor = jnp.linalg.cholesky(pivot_block)
    solved = jax.scipy.linalg.cho_solve((factor, True), row_panel)
    weight_panel = lax.dynamic_slice_in_dim(weights, first_col, pair_width, 1)
    highest = lax.Precision.HIGHEST
    new_matrix = matrix - jnp.dot(column_panel, solved, precision=highest)
    new_weights = weights - jnp.dot(weight_panel, solved, precision=highest)
    return (new_matrix, new_weights)

def reference(hessian, weight, pairs):
    carried = weight.astype(jnp.float32)
    hessian_one, carried = prune_pair(hessian, carried, pairs[0])
    pruned_hessian, carried_two = prune_pair(hessian_one, carried, pairs[1])
    return (pruned_hessian, carried_two.astype(jnp.bfloat16))
```

```python
import functools

import jax
import jax.numpy as jnp
from jax import lax
from jax.experimental import pallas as pl
from jax.experimental.pallas import tpu as pltpu
from jax.sharding import PartitionSpec as P

HEAD = 192
PAIR = 2 * HEAD
NPAIRS = 48
N = 16
LAST = N - 1
MESH = pl.DeviceIdType.MESH
F32 = jnp.float32
BF16 = jnp.bfloat16
ANY = pl.BlockSpec(memory_space=pl.ANY)
VM = pl.BlockSpec(memory_space=pltpu.VMEM)


def remote(src, dst, send, recv, where):
    return pltpu.make_async_remote_copy(
        src_ref=src, dst_ref=dst, send_sem=send, recv_sem=recv,
        device_id=where, device_id_type=MESH,
    )


def greet_groups():
    row, wide = lax.axis_index("row"), lax.axis_index("wide")
    barrier = pltpu.get_barrier_semaphore()

    def body(d, _):
        pl.semaphore_signal(
            barrier, inc=1, device_id={"row": lax.rem(row + d, N)}, device_id_type=MESH
        )
        pl.semaphore_signal(
            barrier, inc=1, device_id={"wide": lax.rem(wide + d, N)}, device_id_type=MESH
        )
        return 0

    lax.fori_loop(1, N, body, 0)
    pl.semaphore_wait(barrier, 2 * (N - 1))


def scatter_kernel(root, cq, wq, pq, rq, c7, w7, r7,
                   ocq, owq, orq, oc7, ow7, or7, opv, pst, ssem, rsem, lsem):
    row, wide = lax.axis_index("row"), lax.axis_index("wide")
    greet_groups()
    at_wide, at_row = wide == root, row == root
    last_wide, last_row = wide == LAST, row == LAST

    def corner(ref):
        return lambda m: ref.at[m, :, pl.ds(2 * PAIR, PAIR)]

    jobs = [
        (0, jnp.logical_and(at_row, at_wide), at_row, "wide", wide, lambda m: pq.at[m], pst.at[0]),
        (1, jnp.logical_and(at_row, last_wide), at_row, "wide", wide, corner(rq), pst.at[1]),
        (2, jnp.logical_and(last_row, last_wide), last_row, "wide", wide, corner(r7), pst.at[2]),
        (3, at_row, None, "row", row, lambda m: rq.at[m], orq),
        (4, last_row, None, "row", row, lambda m: r7.at[m], or7),
        (5, at_wide, None, "wide", wide, lambda m: cq.at[m], ocq),
        (6, last_wide, None, "wide", wide, lambda m: c7.at[m], oc7),
        (7, at_wide, None, "wide", wide, lambda m: wq.at[m], owq),
        (8, last_wide, None, "wide", wide, lambda m: w7.at[m], ow7),
    ]

    def spread(job, act):
        k, mine, _, axis, me, src, dst = job

        @pl.when(mine)
        def _():
            def body(m, _):
                @pl.when(m != me)
                def _():
                    copy = remote(src(m), dst, ssem.at[k, m], rsem.at[k], {axis: m})
                    copy.start() if act == "start" else copy.wait_send()

                @pl.when(m == me)
                def _():
                    copy = pltpu.make_async_copy(src(m), dst, lsem.at[k])
                    copy.start() if act == "start" else copy.wait()
                return 0

            lax.fori_loop(0, N, body, 0)

    def arrive(job):
        k, mine, group, axis, me, src, dst = job
        away = jnp.logical_not(mine)
        if group is not None:
            away = jnp.logical_and(away, group)

        @pl.when(away)
        def _():
            remote(src(0), dst, ssem.at[k, 0], rsem.at[k], {axis: 0}).wait_recv()

    for job in jobs:
        spread(job, "start")
    for job in jobs[:3]:
        arrive(job)
        spread(job, "drain")
    second = [(9, at_row, 0, 0, root), (10, at_row, 1, 0, root), (11, last_row, 2, 1, LAST)]

    def forward(item, act):
        k, mine, part, core, origin = item

        @pl.when(mine)
        def _():
            def body(h, _):
                m = 2 * h + core

                @pl.when(m != origin)
                def _():
                    copy = remote(pst.at[part], opv.at[part], ssem.at[k, m], rsem.at[k], {"row": m})
                    copy.start() if act == "start" else copy.wait_send()

                @pl.when(m == origin)
                def _():
                    copy = pltpu.make_async_copy(pst.at[part], opv.at[part], lsem.at[k])
                    copy.start() if act == "start" else copy.wait()
                return 0

            lax.fori_loop(0, N // 2, body, 0)

    for item in second:
        forward(item, "start")
    for item in second:
        k, mine, part, core, origin = item
        away = jnp.logical_and(jnp.logical_not(mine), lax.rem(row, 2) == core)

        @pl.when(away)
        def _():
            remote(pst.at[part], opv.at[part], ssem.at[k, 0], rsem.at[k], {"row": 0}).wait_recv()

    for job in jobs[3:]:
        arrive(job)
    for item in second:
        forward(item, "drain")
    for job in jobs[3:]:
        spread(job, "drain")


def piece(dtype, *shape):
    return jax.ShapeDtypeStruct(shape, dtype)


PIECES = [
    piece(BF16, 72, PAIR), piece(BF16, 18, PAIR), piece(F32, 24, 1152),
    piece(BF16, 72, PAIR), piece(BF16, 18, PAIR), piece(F32, 24, 1152),
    piece(F32, 3, 24, PAIR),
]


def scatter(root, *operands):
    outs = PIECES + [piece(F32, 3, 24, PAIR)]
    return pl.pallas_call(
        functools.partial(scatter_kernel, root),
        name=f"scatter_{root}",
        out_shape=outs,
        in_specs=[ANY] * 7,
        out_specs=[ANY] * 8,
        scratch_shapes=[
            pltpu.SemaphoreType.DMA((12, N)),
            pltpu.SemaphoreType.DMA((12,)),
            pltpu.SemaphoreType.DMA((12,)),
        ],
        compiler_params=pltpu.CompilerParams(collective_id=1 + root, has_side_effects=True),
    )(*operands)[:7]


def gather_kernel(cq, wq, rq, c7, w7, r7, pv,
                  gcq, gwq, grq, gc7, gw7, gr7, gpv, ssem, rsem, lsem, fsem, gsem):
    row, wide = lax.axis_index("row"), lax.axis_index("wide")
    core = lax.rem(row, 2)
    greet_groups()
    along_wide = [(0, cq, gcq), (1, c7, gc7), (2, wq, gwq), (3, w7, gw7)]
    along_row = [(4, rq, grq), (5, r7, gr7)]
    pivots = [(6, pv.at[0], gpv.at[0], 0), (7, pv.at[1], gpv.at[1], 0), (8, pv.at[2], gpv.at[2], 1)]

    def wide_copy(k, src, dst, d):
        return remote(src, dst.at[wide], ssem.at[k, d], rsem.at[k, d], {"wide": lax.rem(wide + d, N)})

    def wide_arrival(k, src, dst, d):
        return remote(src, dst.at[lax.rem(wide + N - d, N)], ssem.at[k, d], rsem.at[k, d],
                      {"wide": lax.rem(wide + d, N)})

    def row_copy(k, src, dst, d):
        return remote(src, dst.at[row], ssem.at[k, d], rsem.at[k, d], {"row": lax.rem(row + d, N)})

    def row_arrival(k, src, dst, d):
        return remote(src, dst.at[lax.rem(row + N - d, N)], ssem.at[k, d], rsem.at[k, d],
                      {"row": lax.rem(row + d, N)})

    def over(n, f):
        def body(d, _):
            f(d)
            return 0
        lax.fori_loop(1, n, body, 0)

    for k, src, dst, c in pivots:
        @pl.when(core == c)
        def _():
            pltpu.make_async_copy(src, dst.at[wide], lsem.at[k]).start()
            over(N, lambda d: wide_copy(k, src, dst, d).start())
    for k, src, dst in along_row:
        pltpu.make_async_copy(src, dst.at[row], lsem.at[k]).start()
        over(N // 2, lambda d: row_copy(k, src, dst, 2 * d).start())
    for k, src, dst in along_wide:
        pltpu.make_async_copy(src, dst.at[wide], lsem.at[k]).start()
        over(N, lambda d: wide_copy(k, src, dst, d).start())

    partner = {"row": row + 1 - 2 * core}
    for k, src, dst, c in pivots:
        @pl.when(core == c)
        def _():
            pltpu.make_async_copy(src, dst.at[wide], lsem.at[k]).wait()
            over(N, lambda d: wide_arrival(k, src, dst, d).wait_recv())
            remote(dst, dst, fsem.at[k - 6], gsem.at[k - 6], partner).start()
    for k, src, dst in along_row:
        pltpu.make_async_copy(src, dst.at[row], lsem.at[k]).wait()

    def relay(k, dst, d):
        block = dst.at[lax.rem(row + N - 2 * d, N)]
        return remote(block, block, fsem.at[3 + (k - 4) * 8 + d], gsem.at[3 + (k - 4) * 8 + d], partner)

    def relayed(k, dst, d):
        block = dst.at[lax.rem(row + 1 - 2 * core + N - 2 * d, N)]
        return remote(block, block, fsem.at[3 + (k - 4) * 8 + d], gsem.at[3 + (k - 4) * 8 + d], partner)

    for k, src, dst in along_row:
        relay(k, dst, 0).start()

        def step(d):
            row_arrival(k, src, dst, 2 * d).wait_recv()
            relay(k, dst, d).start()
        over(N // 2, step)
    for k, src, dst in along_wide:
        pltpu.make_async_copy(src, dst.at[wide], lsem.at[k]).wait()
        over(N, lambda d: wide_arrival(k, src, dst, d).wait_recv())
    for k, src, dst, c in pivots:
        @pl.when(core != c)
        def _():
            remote(dst, dst, fsem.at[k - 6], gsem.at[k - 6], partner).wait_recv()

        @pl.when(core == c)
        def _():
            remote(dst, dst, fsem.at[k - 6], gsem.at[k - 6], partner).wait_send()
            over(N, lambda d: wide_copy(k, src, dst, d).wait_send())
    for k, src, dst in along_row:
        def finish(d):
            relayed(k, dst, d).wait_recv()
            relay(k, dst, d).wait_send()
        finish(0)
        over(N // 2, finish)
        over(N // 2, lambda d: row_copy(k, src, dst, 2 * d).wait_send())
    for k, src, dst in along_wide:
        over(N, lambda d: wide_copy(k, src, dst, d).wait_send())


def gather(pieces):
    outs = [piece(p.dtype, N, *p.shape) for p in PIECES[:6]] + [piece(F32, 3, N, 24, PAIR)]
    return pl.pallas_call(
        gather_kernel,
        name="gather_panels",
        out_shape=outs,
        in_specs=[ANY] * 7,
        out_specs=[ANY] * 7,
        scratch_shapes=[
            pltpu.SemaphoreType.DMA((9, N)),
            pltpu.SemaphoreType.DMA((9, N)),
            pltpu.SemaphoreType.DMA((9,)),
            pltpu.SemaphoreType.DMA((19,)),
            pltpu.SemaphoreType.DMA((19,)),
        ],
        compiler_params=pltpu.CompilerParams(collective_id=0, has_side_effects=True),
    )(*pieces)


def dot(a, b):
    return jnp.dot(a, b, preferred_element_type=F32)


def split(a):
    high = a.astype(BF16)
    return high, (a - high.astype(F32)).astype(BF16)


def dot3(a, b):
    ah, al = split(a)
    bh, bl = split(b)
    return dot(ah, bh) + (dot(ah, bl) + dot(al, bh))


def invert(a_ref, out_ref, s_ref, x_ref, r_ref):
    n = PAIR
    eye = (
        lax.broadcasted_iota(jnp.int32, (n, n), 0) == lax.broadcasted_iota(jnp.int32, (n, n), 1)
    ).astype(F32)
    a = a_ref[...]
    across = lax.rsqrt(jnp.sum(a * eye, axis=0, keepdims=True))
    down = lax.rsqrt(jnp.sum(a * eye, axis=1, keepdims=True))
    s_ref[...] = a * across * down
    bound = jnp.max(jnp.sum(jnp.abs(s_ref[...]), axis=1, keepdims=True), axis=0, keepdims=True)
    start = 1.9 / bound
    x_ref[...] = start * eye
    r_ref[...] = eye - start * s_ref[...]

    def quick(_, c):
        r = r_ref[...].astype(BF16)
        x = x_ref[...]
        x_ref[...] = x + dot(x.astype(BF16), r)
        r_ref[...] = dot(r, r)
        return c

    lax.fori_loop(0, 6, quick, 0)

    def careful(state):
        step, _ = state
        r = eye - dot3(s_ref[...], x_ref[...])
        size = jnp.max(jnp.sum(jnp.abs(r), axis=1, keepdims=True))
        lost = jnp.logical_and(step == 0, jnp.logical_not(size < 0.9))
        r_ref[...] = r

        @pl.when(lost)
        def _():
            x_ref[...] = eye / bound

        @pl.when(jnp.logical_not(lost))
        def _():
            x = x_ref[...]
            x_ref[...] = x + dot3(x, r_ref[...])

        return step + 1, jnp.where(lost, 1.0, size)

    lax.while_loop(lambda s: jnp.logical_and(s[0] < 64, s[1] > 3e-4), careful, (0, 1.0))
    out_ref[...] = x_ref[...] * across * down


def factor_kernel(pv, ga, gb, t, s_ref, x_ref, r_ref, c_ref):
    invert(pv.at[0], ga, s_ref, x_ref, r_ref)
    cross = pv[1]
    t[...] = dot3(ga[...], cross)
    c_ref[...] = pv[2] - dot3(cross.T, t[...])
    invert(c_ref, gb, s_ref, x_ref, r_ref)


def factor(pv):
    block = piece(F32, PAIR, PAIR)
    return pl.pallas_call(
        factor_kernel,
        name="factor",
        out_shape=[block] * 3,
        in_specs=[VM],
        out_specs=[VM] * 3,
        scratch_shapes=[pltpu.VMEM((PAIR, PAIR), F32)] * 4,
    )(pv)


def per_device(hessian, weight, pairs):
    tile = hessian.shape[0]
    per_tile = tile // PAIR
    other = jnp.minimum(pairs[0], pairs[1])
    root = other // per_tile
    start = (other % per_tile) * PAIR
    last = (per_tile - 1) * PAIR

    cq = lax.dynamic_slice_in_dim(hessian, start, PAIR, 1)
    wq = lax.dynamic_slice_in_dim(weight, start, PAIR, 1)
    rq = lax.dynamic_slice_in_dim(hessian, start, PAIR, 0)
    pq = lax.dynamic_slice_in_dim(rq, start, PAIR, 1)
    c7 = hessian[:, last:]
    w7 = weight[:, last:]
    r7 = hessian[last:, :]
    operands = (
        cq.astype(BF16).reshape(N, 72, PAIR), wq.reshape(N, 18, PAIR), pq.reshape(N, 24, PAIR),
        rq.reshape(N, 24, tile), c7.astype(BF16).reshape(N, 72, PAIR), w7.reshape(N, 18, PAIR),
        r7.reshape(N, 24, tile),
    )
    pieces = lax.switch(root, [functools.partial(scatter, i) for i in range(N)], *operands)
    gcq, gwq, grq, gc7, gw7, gr7, gpv = gather(pieces)

    inv_a, inv_b, t = factor(gpv.reshape(3, PAIR, PAIR))
    high = lax.Precision.HIGH
    b0, b1 = grq.reshape(PAIR, tile), gr7.reshape(PAIR, tile)
    xa0 = jnp.dot(inv_a, b0, precision=high)
    rest = b1 - lax.dot_general(
        gpv.reshape(3, PAIR, PAIR)[1], xa0, (((0,), (0,)), ((), ())), precision=high
    )
    xb = jnp.dot(inv_b, rest, precision=high)
    xa = xa0 - jnp.dot(t, xb, precision=high)
    x = jnp.concatenate([xa, xb], 0)
    panel = jnp.concatenate([gcq.reshape(tile, PAIR), gc7.reshape(tile, PAIR)], 1)
    xh32 = lax.reduce_precision(x, 8, 7)
    xh, xl = xh32.astype(BF16), (x - xh32).astype(BF16)

    def pruned(axis, shape, dim):
        block = (lax.axis_index(axis) * tile + lax.broadcasted_iota(jnp.int32, shape, dim)) // PAIR
        return jnp.logical_or(block == other, block == NPAIRS - 1)

    gone = jnp.logical_or(pruned("row", (tile, 1), 0), pruned("wide", (1, tile), 1))
    pruned_hessian = jnp.where(gone, 0.0, hessian - dot(panel, xh))
    rows = weight.shape[0]
    wp = jnp.concatenate([gwq.reshape(rows, PAIR), gw7.reshape(rows, PAIR)], 1)
    pruned_weight = (weight.astype(F32) - (dot(wp, xh) + dot(wp, xl))).astype(BF16)
    return pruned_hessian, pruned_weight


def solution(mesh):
    return jax.shard_map(
        per_device,
        mesh=mesh,
        in_specs=(P("row", "wide"), P("row", "wide"), P()),
        out_specs=(P("row", "wide"), P("row", "wide")),
        check_vma=False,
    )
```

```python
import functools

import jax
import jax.numpy as jnp
from jax import lax
from jax.experimental import pallas as pl
from jax.experimental.pallas import tpu as pltpu
from jax.sharding import PartitionSpec as P

HEAD = 192
PAIR = 2 * HEAD
NPAIRS = 48
N = 16
LAST = N - 1
MESH = pl.DeviceIdType.MESH
F32 = jnp.float32
BF16 = jnp.bfloat16
ANY = pl.BlockSpec(memory_space=pl.ANY)
VM = pl.BlockSpec(memory_space=pltpu.VMEM)


def remote(src, dst, send, recv, where):
    return pltpu.make_async_remote_copy(
        src_ref=src, dst_ref=dst, send_sem=send, recv_sem=recv,
        device_id=where, device_id_type=MESH,
    )


def greet_groups():
    row, wide = lax.axis_index("row"), lax.axis_index("wide")
    barrier = pltpu.get_barrier_semaphore()

    def body(d, _):
        pl.semaphore_signal(
            barrier, inc=1, device_id={"row": lax.rem(row + d, N)}, device_id_type=MESH
        )
        pl.semaphore_signal(
            barrier, inc=1, device_id={"wide": lax.rem(wide + d, N)}, device_id_type=MESH
        )
        return 0

    lax.fori_loop(1, N, body, 0)
    pl.semaphore_wait(barrier, 2 * (N - 1))


def scatter_kernel(root, cq, wq, pq, rq, c7, w7, r7,
                   ocq, owq, orq, oc7, ow7, or7, opv, pst, ssem, rsem, lsem):
    row, wide = lax.axis_index("row"), lax.axis_index("wide")
    greet_groups()
    at_wide, at_row = wide == root, row == root
    last_wide, last_row = wide == LAST, row == LAST

    def strip(m, columns):
        return r7.at[pl.ds(pl.multiple_of(2 * PAIR + 24 * m, 8), 24), columns]

    jobs = [
        (0, jnp.logical_and(at_row, at_wide), at_row, "wide", wide, lambda m: pq.at[m], pst.at[0]),
        (1, jnp.logical_and(at_row, last_wide), at_row, "wide", wide, lambda m: rq.at[m, :, pl.ds(2 * PAIR, PAIR)], pst.at[1]),
        (2, jnp.logical_and(last_row, last_wide), last_row, "wide", wide, lambda m: strip(m, pl.ds(2 * PAIR, PAIR)), pst.at[2]),
        (3, at_row, None, "row", row, lambda m: rq.at[m], orq),
        (4, last_row, None, "row", row, lambda m: strip(m, slice(None)), or7),
        (5, at_wide, None, "wide", wide, lambda m: cq.at[m], ocq),
        (6, last_wide, None, "wide", wide, lambda m: c7.at[m], oc7),
        (7, at_wide, None, "wide", wide, lambda m: wq.at[m], owq),
        (8, last_wide, None, "wide", wide, lambda m: w7.at[m], ow7),
    ]

    def spread(job, act):
        k, mine, _, axis, me, src, dst = job

        @pl.when(mine)
        def _():
            def body(m, _):
                @pl.when(m != me)
                def _():
                    copy = remote(src(m), dst, ssem.at[k, m], rsem.at[k], {axis: m})
                    copy.start() if act == "start" else copy.wait_send()

                @pl.when(m == me)
                def _():
                    copy = pltpu.make_async_copy(src(m), dst, lsem.at[k])
                    copy.start() if act == "start" else copy.wait()
                return 0

            lax.fori_loop(0, N, body, 0)

    def arrive(job):
        k, mine, group, axis, me, src, dst = job
        away = jnp.logical_not(mine)
        if group is not None:
            away = jnp.logical_and(away, group)

        @pl.when(away)
        def _():
            remote(src(0), dst, ssem.at[k, 0], rsem.at[k], {axis: 0}).wait_recv()

    for job in jobs:
        spread(job, "start")
    for job in jobs[:3]:
        arrive(job)
        spread(job, "drain")
    second = [(9, at_row, 0, 0, root), (10, at_row, 1, 0, root), (11, last_row, 2, 1, LAST)]

    def forward(item, act):
        k, mine, part, core, origin = item

        @pl.when(mine)
        def _():
            def body(h, _):
                m = 2 * h + core

                @pl.when(m != origin)
                def _():
                    copy = remote(pst.at[part], opv.at[part], ssem.at[k, m], rsem.at[k], {"row": m})
                    copy.start() if act == "start" else copy.wait_send()

                @pl.when(m == origin)
                def _():
                    copy = pltpu.make_async_copy(pst.at[part], opv.at[part], lsem.at[k])
                    copy.start() if act == "start" else copy.wait()
                return 0

            lax.fori_loop(0, N // 2, body, 0)

    for item in second:
        forward(item, "start")
    for item in second:
        k, mine, part, core, origin = item
        away = jnp.logical_and(jnp.logical_not(mine), lax.rem(row, 2) == core)

        @pl.when(away)
        def _():
            remote(pst.at[part], opv.at[part], ssem.at[k, 0], rsem.at[k], {"row": 0}).wait_recv()

    for job in jobs[3:]:
        arrive(job)
    for item in second:
        forward(item, "drain")
    for job in jobs[3:]:
        spread(job, "drain")


def piece(dtype, *shape):
    return jax.ShapeDtypeStruct(shape, dtype)


PIECES = [
    piece(BF16, 72, PAIR), piece(BF16, 18, PAIR), piece(F32, 24, 1152),
    piece(BF16, 72, PAIR), piece(BF16, 18, PAIR), piece(F32, 24, 1152),
    piece(F32, 3, 24, PAIR),
]


def scatter(root, *operands):
    outs = PIECES + [piece(F32, 3, 24, PAIR)]
    return pl.pallas_call(
        functools.partial(scatter_kernel, root),
        name=f"scatter_{root}",
        out_shape=outs,
        in_specs=[ANY] * 7,
        out_specs=[ANY] * 8,
        scratch_shapes=[
            pltpu.SemaphoreType.DMA((12, N)),
            pltpu.SemaphoreType.DMA((12,)),
            pltpu.SemaphoreType.DMA((12,)),
        ],
        compiler_params=pltpu.CompilerParams(collective_id=1 + root, has_side_effects=True),
    )(*operands)[:7]


def gather_kernel(cq, wq, rq, c7, w7, r7, pv,
                  gcq, gwq, grq, gc7, gw7, gr7, gpv,
                  lsem, xs, xr, zs, zr, hs, hr, ps, pr, fs, fr):
    row, wide = lax.axis_index("row"), lax.axis_index("wide")
    core, x, upper = lax.rem(row, 2), lax.rem(row // 2, 4), row // 8
    y, z = wide // 8, lax.rem(wide, 8)

    def on_wide(t, dz):
        return lax.rem(y + t, 2) * 8 + lax.rem(z + dz + 8, 8)

    def on_row(t, dx, other=0):
        chip = lax.rem(upper + t, 2) * 4 + lax.rem(x + dx + 4, 4)
        return chip * 2 + (core if other == 0 else 1 - core)

    neighbours = [
        {"wide": on_wide(0, 1)}, {"wide": on_wide(0, -1)}, {"wide": on_wide(1, 0)},
        {"row": on_row(0, 1)}, {"row": on_row(0, -1)}, {"row": on_row(1, 0)}, {"row": on_row(0, 0, 1)},
    ]
    barrier = pltpu.get_barrier_semaphore()
    for where in neighbours:
        pl.semaphore_signal(barrier, inc=1, device_id=where, device_id_type=MESH)
    pl.semaphore_wait(barrier, len(neighbours))
    partner = {"row": on_row(0, 0, 1)}

    pivots = [(0, pv.at[0], gpv.at[0], 0, 0), (1, pv.at[1], gpv.at[1], 1, 0), (2, pv.at[2], gpv.at[2], 0, 1)]
    columns = [(3, cq, gcq, 0, None), (4, c7, gc7, 1, None), (5, wq, gwq, 0, None), (6, w7, gw7, 1, None)]
    rows = [(7, rq, grq, 0, None), (8, r7, gr7, 1, None)]
    sign = (1, -1)

    def only(job, f):
        if job[4] is None:
            f()
        else:
            pl.when(core == job[4])(f)

    def local(job):
        k, src, dst = job[:3]
        return pltpu.make_async_copy(src, dst.at[row if k >= 7 else wide], lsem.at[k])

    def across(job):
        k, src, dst = job[:3]
        if k >= 7:
            return remote(src, dst.at[row], xs.at[k], xr.at[k], {"row": on_row(1, 0)})
        return remote(src, dst.at[wide], xs.at[k], xr.at[k], {"wide": on_wide(1, 0)})

    def crossed(job):
        k, src, dst = job[:3]
        if k >= 7:
            return remote(src, dst.at[on_row(1, 0)], xs.at[k], xr.at[k], {"row": on_row(1, 0)})
        return remote(src, dst.at[on_wide(1, 0)], xs.at[k], xr.at[k], {"wide": on_wide(1, 0)})

    def hop(job, t, way, d, arriving=False):
        k, src, dst = job[:3]
        s = sign[way]
        back = d if arriving else d - 1
        if k >= 7:
            block = dst.at[on_row(t, -s * back)]
            start = src if isinstance(d, int) and d == 1 and t == 0 else block
            return remote(start, block, hs.at[k - 7, t, way, d], hr.at[k - 7, t, way, d], {"row": on_row(0, s)})
        block = dst.at[on_wide(t, -s * back)]
        start = src if isinstance(d, int) and d == 1 and t == 0 else block
        return remote(start, block, zs.at[k, t, way, d], zr.at[k, t, way, d], {"wide": on_wide(0, s)})

    def share(job, t, dx, arriving=False):
        k, src, dst = job[:3]
        block = dst.at[on_row(t, dx, 1 if arriving else 0)]
        rel = dx + 2
        return remote(block, block, fs.at[k - 7, t, rel], fr.at[k - 7, t, rel], partner)

    def begin(job):
        local(job).start()
        across(job).start()
        hop(job, 0, 0, 1).start()
        hop(job, 0, 1, 1).start()

    def second(job):
        crossed(job).wait_recv()
        hop(job, 1, 0, 1).start()
        hop(job, 1, 1, 1).start()

    def pass_on(job, d, ways):
        for t in (0, 1):
            for way in (0, 1):
                hop(job, t, way, d, True).wait_recv()
                if ways == 2 or (ways == 1 and way == job[3]):
                    hop(job, t, way, d + 1).start()

    def last(job, d):
        for t in (0, 1):
            hop(job, t, job[3], d, True).wait_recv()

    for job in pivots + rows + columns:
        only(job, lambda: begin(job))
    for job in rows:
        local(job).wait()
        share(job, 0, 0).start()
    for job in pivots:
        only(job, lambda: second(job))
    for job in rows:
        second(job)
        share(job, 1, 0).start()
    for job in columns:
        second(job)

    def middle(d, with_rows):
        for job in pivots:
            only(job, lambda: pass_on(job, d, 2 if d < 3 else 1))
        if with_rows:
            for job in rows:
                if d == 1:
                    pass_on(job, 1, 1)
                    for t in (0, 1):
                        share(job, t, -1).start()
                        share(job, t, 1).start()
                elif d == 2:
                    last(job, 2)
                    for t in (0, 1):
                        share(job, t, -2).start()
        for job in columns:
            pass_on(job, d, 2 if d < 3 else 1)

    for d in (1, 2, 3):
        middle(d, d < 3)
    for job in pivots:
        def done(job=job):
            local(job).wait()
            last(job, 4)
            remote(job[2], job[2], ps.at[job[0]], pr.at[job[0]], partner).start()
        only(job, done)
    for job in columns:
        local(job).wait()
        last(job, 4)

    def sent(job):
        across(job).wait_send()
        full = 2 if job[0] >= 7 else 4
        for t in (0, 1):
            for way in (0, 1):
                for d in range(1, full + 1 if way == job[3] else full):
                    hop(job, t, way, d).wait_send()

    for job in pivots:
        def carried(job=job):
            sent(job)
            remote(job[2], job[2], ps.at[job[0]], pr.at[job[0]], partner).wait_send()
        only(job, carried)

        @pl.when(core != job[4])
        def _():
            remote(job[2], job[2], ps.at[job[0]], pr.at[job[0]], partner).wait_recv()
    for job in columns:
        sent(job)
    for job in rows:
        sent(job)
        for t in (0, 1):
            for dx in (0, -1, 1, -2):
                share(job, t, dx, True).wait_recv()
                share(job, t, dx).wait_send()


def gather(pieces):
    outs = [piece(p.dtype, N, *p.shape) for p in PIECES[:6]] + [piece(F32, 3, N, 24, PAIR)]
    return pl.pallas_call(
        gather_kernel,
        name="gather_panels",
        out_shape=outs,
        in_specs=[ANY] * 7,
        out_specs=[ANY] * 7,
        scratch_shapes=[
            pltpu.SemaphoreType.DMA((9,)),
            pltpu.SemaphoreType.DMA((9,)),
            pltpu.SemaphoreType.DMA((9,)),
            pltpu.SemaphoreType.DMA((7, 2, 2, 5)),
            pltpu.SemaphoreType.DMA((7, 2, 2, 5)),
            pltpu.SemaphoreType.DMA((2, 2, 2, 3)),
            pltpu.SemaphoreType.DMA((2, 2, 2, 3)),
            pltpu.SemaphoreType.DMA((3,)),
            pltpu.SemaphoreType.DMA((3,)),
            pltpu.SemaphoreType.DMA((2, 2, 4)),
            pltpu.SemaphoreType.DMA((2, 2, 4)),
        ],
        compiler_params=pltpu.CompilerParams(collective_id=0, has_side_effects=True),
    )(*pieces)


def dot(a, b):
    return jnp.dot(a, b, preferred_element_type=F32)


def split(a):
    high = a.astype(BF16)
    return high, (a - high.astype(F32)).astype(BF16)


def dot3(a, b):
    ah, al = split(a)
    bh, bl = split(b)
    return dot(ah, bh) + (dot(ah, bl) + dot(al, bh))


def invert(a_ref, out_ref, s_ref, x_ref, r_ref):
    n = PAIR
    eye = (
        lax.broadcasted_iota(jnp.int32, (n, n), 0) == lax.broadcasted_iota(jnp.int32, (n, n), 1)
    ).astype(F32)
    a = a_ref[...]
    across = lax.rsqrt(jnp.sum(a * eye, axis=0, keepdims=True))
    down = lax.rsqrt(jnp.sum(a * eye, axis=1, keepdims=True))
    s_ref[...] = a * across * down
    bound = jnp.max(jnp.sum(jnp.abs(s_ref[...]), axis=1, keepdims=True), axis=0, keepdims=True)
    start = 1.9 / bound
    x_ref[...] = start * eye
    r_ref[...] = eye - start * s_ref[...]

    def quick(_, c):
        r = r_ref[...].astype(BF16)
        x = x_ref[...]
        x_ref[...] = x + dot(x.astype(BF16), r)
        r_ref[...] = dot(r, r)
        return c

    lax.fori_loop(0, 6, quick, 0)

    def careful(state):
        step, _ = state
        r = eye - dot3(s_ref[...], x_ref[...])
        size = jnp.max(jnp.sum(jnp.abs(r), axis=1, keepdims=True))
        lost = jnp.logical_and(step == 0, jnp.logical_not(size < 0.9))
        r_ref[...] = r

        @pl.when(lost)
        def _():
            x_ref[...] = eye / bound

        @pl.when(jnp.logical_not(lost))
        def _():
            x = x_ref[...]
            x_ref[...] = x + dot3(x, r_ref[...])

        return step + 1, jnp.where(lost, 1.0, size)

    lax.while_loop(lambda s: jnp.logical_and(s[0] < 64, s[1] > 3e-4), careful, (0, 1.0))
    out_ref[...] = x_ref[...] * across * down


def factor_kernel(pv, ga, gb, t, s_ref, x_ref, r_ref, c_ref):
    invert(pv.at[0], ga, s_ref, x_ref, r_ref)
    cross = pv[1]
    t[...] = dot3(ga[...], cross)
    c_ref[...] = pv[2] - dot3(cross.T, t[...])
    invert(c_ref, gb, s_ref, x_ref, r_ref)


def factor(pv):
    block = piece(F32, PAIR, PAIR)
    return pl.pallas_call(
        factor_kernel,
        name="factor",
        out_shape=[block] * 3,
        in_specs=[VM],
        out_specs=[VM] * 3,
        scratch_shapes=[pltpu.VMEM((PAIR, PAIR), F32)] * 4,
    )(pv)


def cut_kernel(block, hc, hr, hp, h7, wc, w7, ocq, owq, opq, orq, oc7, ow7):
    for m in range(N // 2):
        ocq[m] = hc[72 * m : 72 * m + 72, :].astype(BF16)
        oc7[m] = h7[72 * m : 72 * m + 72, :].astype(BF16)
        orq[m] = hr[24 * m : 24 * m + 24, :]
        opq[m] = hp[24 * m : 24 * m + 24, :]
    for src, out in ((wc, owq), (w7, ow7)):
        full = src[...].astype(F32)
        for m in range(N // 2):
            out[m] = full[18 * m : 18 * m + 18, :].astype(BF16)


def cut(block, hessian, weight):
    half = N // 2

    def out(*shape):
        return pl.BlockSpec((half, *shape), lambda g, b: (g, 0, 0))

    return pl.pallas_call(
        cut_kernel,
        name="cut",
        out_shape=[
            piece(BF16, N, 72, PAIR), piece(BF16, N, 18, PAIR), piece(F32, N, 24, PAIR),
            piece(F32, N, 24, 1152), piece(BF16, N, 72, PAIR), piece(BF16, N, 18, PAIR),
        ],
        grid_spec=pltpu.PrefetchScalarGridSpec(
            num_scalar_prefetch=1,
            grid=(2,),
            in_specs=[
                pl.BlockSpec((576, PAIR), lambda g, b: (g, b[0])),
                pl.BlockSpec((192, 1152), lambda g, b: (2 * b[0] + g, 0)),
                pl.BlockSpec((192, PAIR), lambda g, b: (2 * b[0] + g, b[0])),
                pl.BlockSpec((576, PAIR), lambda g, b: (g, 2)),
                pl.BlockSpec((144, PAIR), lambda g, b: (g, b[0])),
                pl.BlockSpec((144, PAIR), lambda g, b: (g, 2)),
            ],
            out_specs=[out(72, PAIR), out(18, PAIR), out(24, PAIR), out(24, 1152), out(72, PAIR), out(18, PAIR)],
        ),
    )(block, hessian, hessian, hessian, hessian, weight, weight)


def per_device(hessian, weight, pairs):
    tile = hessian.shape[0]
    per_tile = tile // PAIR
    other = jnp.minimum(pairs[0], pairs[1])
    root = other // per_tile
    block = (other % per_tile).reshape(1)
    cq, wq, pq, rq, c7, w7 = cut(block, hessian, weight)
    operands = (cq, wq, pq, rq, c7, w7, hessian)
    pieces = lax.switch(root, [functools.partial(scatter, i) for i in range(N)], *operands)
    gcq, gwq, grq, gc7, gw7, gr7, gpv = gather(pieces)

    inv_a, inv_b, t = factor(gpv.reshape(3, PAIR, PAIR))
    high = lax.Precision.HIGH
    b0, b1 = grq.reshape(PAIR, tile), gr7.reshape(PAIR, tile)
    xa0 = jnp.dot(inv_a, b0, precision=high)
    rest = b1 - lax.dot_general(
        gpv.reshape(3, PAIR, PAIR)[1], xa0, (((0,), (0,)), ((), ())), precision=high
    )
    xb = jnp.dot(inv_b, rest, precision=high)
    xa = xa0 - jnp.dot(t, xb, precision=high)
    x = jnp.concatenate([xa, xb], 0)
    panel = jnp.concatenate([gcq.reshape(tile, PAIR), gc7.reshape(tile, PAIR)], 1)
    xh32 = lax.reduce_precision(x, 8, 7)
    xh, xl = xh32.astype(BF16), (x - xh32).astype(BF16)

    def pruned(axis, shape, dim):
        block = (lax.axis_index(axis) * tile + lax.broadcasted_iota(jnp.int32, shape, dim)) // PAIR
        return jnp.logical_or(block == other, block == NPAIRS - 1)

    gone = jnp.logical_or(pruned("row", (tile, 1), 0), pruned("wide", (1, tile), 1))
    pruned_hessian = jnp.where(gone, 0.0, hessian - dot(panel, xh))
    rows = weight.shape[0]
    wp = jnp.concatenate([gwq.reshape(rows, PAIR), gw7.reshape(rows, PAIR)], 1)
    pruned_weight = (weight.astype(F32) - (dot(wp, xh) + dot(wp, xl))).astype(BF16)
    return pruned_hessian, pruned_weight


def solution(mesh):
    return jax.shard_map(
        per_device,
        mesh=mesh,
        in_specs=(P("row", "wide"), P("row", "wide"), P()),
        out_specs=(P("row", "wide"), P("row", "wide")),
        check_vma=False,
    )
```

```python
import functools

import jax
import jax.numpy as jnp
from jax import lax
from jax.experimental import pallas as pl
from jax.experimental.pallas import tpu as pltpu
from jax.sharding import PartitionSpec as P

HEAD = 192
PAIR = 2 * HEAD
NPAIRS = 48
N = 16
LAST = N - 1
MESH = pl.DeviceIdType.MESH
F32 = jnp.float32
BF16 = jnp.bfloat16
ANY = pl.BlockSpec(memory_space=pl.ANY)
VM = pl.BlockSpec(memory_space=pltpu.VMEM)


def remote(src, dst, send, recv, where):
    return pltpu.make_async_remote_copy(
        src_ref=src, dst_ref=dst, send_sem=send, recv_sem=recv,
        device_id=where, device_id_type=MESH,
    )


def greet_groups():
    row, wide = lax.axis_index("row"), lax.axis_index("wide")
    barrier = pltpu.get_barrier_semaphore()

    def body(d, _):
        pl.semaphore_signal(
            barrier, inc=1, device_id={"row": lax.rem(row + d, N)}, device_id_type=MESH
        )
        pl.semaphore_signal(
            barrier, inc=1, device_id={"wide": lax.rem(wide + d, N)}, device_id_type=MESH
        )
        return 0

    lax.fori_loop(1, N, body, 0)
    pl.semaphore_wait(barrier, 2 * (N - 1))


def scatter_kernel(root, cq, wq, pq, rq, c7, w7, r7,
                   ocq, owq, orq, oc7, ow7, or7, opv, pst, ssem, rsem, lsem):
    row, wide = lax.axis_index("row"), lax.axis_index("wide")
    greet_groups()
    at_wide, at_row = wide == root, row == root
    last_wide, last_row = wide == LAST, row == LAST

    def strip(m, columns):
        return r7.at[pl.ds(pl.multiple_of(2 * PAIR + 24 * m, 8), 24), columns]

    jobs = [
        (0, jnp.logical_and(at_row, at_wide), at_row, "wide", wide, lambda m: pq.at[m], pst.at[0]),
        (1, jnp.logical_and(at_row, last_wide), at_row, "wide", wide, lambda m: rq.at[m, :, pl.ds(2 * PAIR, PAIR)], pst.at[1]),
        (2, jnp.logical_and(last_row, last_wide), last_row, "wide", wide, lambda m: strip(m, pl.ds(2 * PAIR, PAIR)), pst.at[2]),
        (3, at_row, None, "row", row, lambda m: rq.at[m], orq),
        (4, last_row, None, "row", row, lambda m: strip(m, slice(None)), or7),
        (5, at_wide, None, "wide", wide, lambda m: cq.at[m], ocq),
        (6, last_wide, None, "wide", wide, lambda m: c7.at[m], oc7),
        (7, at_wide, None, "wide", wide, lambda m: wq.at[m], owq),
        (8, last_wide, None, "wide", wide, lambda m: w7.at[m], ow7),
    ]

    def spread(job, act):
        k, mine, _, axis, me, src, dst = job

        @pl.when(mine)
        def _():
            def body(m, _):
                @pl.when(m != me)
                def _():
                    copy = remote(src(m), dst, ssem.at[k, m], rsem.at[k], {axis: m})
                    copy.start() if act == "start" else copy.wait_send()

                @pl.when(m == me)
                def _():
                    copy = pltpu.make_async_copy(src(m), dst, lsem.at[k])
                    copy.start() if act == "start" else copy.wait()
                return 0

            lax.fori_loop(0, N, body, 0)

    def arrive(job):
        k, mine, group, axis, me, src, dst = job
        away = jnp.logical_not(mine)
        if group is not None:
            away = jnp.logical_and(away, group)

        @pl.when(away)
        def _():
            remote(src(0), dst, ssem.at[k, 0], rsem.at[k], {axis: 0}).wait_recv()

    for job in jobs:
        spread(job, "start")
    for job in jobs[:3]:
        arrive(job)
        spread(job, "drain")
    second = [(9, at_row, 0, 0, root), (10, at_row, 1, 0, root), (11, last_row, 2, 1, LAST)]

    def forward(item, act):
        k, mine, part, core, origin = item

        @pl.when(mine)
        def _():
            def body(h, _):
                m = 2 * h + core

                @pl.when(m != origin)
                def _():
                    copy = remote(pst.at[part], opv.at[part], ssem.at[k, m], rsem.at[k], {"row": m})
                    copy.start() if act == "start" else copy.wait_send()

                @pl.when(m == origin)
                def _():
                    copy = pltpu.make_async_copy(pst.at[part], opv.at[part], lsem.at[k])
                    copy.start() if act == "start" else copy.wait()
                return 0

            lax.fori_loop(0, N // 2, body, 0)

    for item in second:
        forward(item, "start")
    for item in second:
        k, mine, part, core, origin = item
        away = jnp.logical_and(jnp.logical_not(mine), lax.rem(row, 2) == core)

        @pl.when(away)
        def _():
            remote(pst.at[part], opv.at[part], ssem.at[k, 0], rsem.at[k], {"row": 0}).wait_recv()

    for job in jobs[3:]:
        arrive(job)
    for item in second:
        forward(item, "drain")
    for job in jobs[3:]:
        spread(job, "drain")


def piece(dtype, *shape):
    return jax.ShapeDtypeStruct(shape, dtype)


PIECES = [
    piece(BF16, 72, PAIR), piece(BF16, 18, PAIR), piece(F32, 24, 1152),
    piece(BF16, 72, PAIR), piece(BF16, 18, PAIR), piece(F32, 24, 1152),
    piece(F32, 3, 24, PAIR),
]


def scatter(root, *operands):
    outs = PIECES + [piece(F32, 3, 24, PAIR)]
    return pl.pallas_call(
        functools.partial(scatter_kernel, root),
        name=f"scatter_{root}",
        out_shape=outs,
        in_specs=[ANY] * 7,
        out_specs=[ANY] * 8,
        scratch_shapes=[
            pltpu.SemaphoreType.DMA((12, N)),
            pltpu.SemaphoreType.DMA((12,)),
            pltpu.SemaphoreType.DMA((12,)),
        ],
        compiler_params=pltpu.CompilerParams(collective_id=1 + root, has_side_effects=True),
    )(*operands)[:7]


def gather_kernel(cq, wq, rq, c7, w7, r7, pv,
                  gcq, gwq, grq, gc7, gw7, gr7, gpv,
                  lsem, xs, xr, zs, zr, hs, hr, ps, pr, fs, fr):
    row, wide = lax.axis_index("row"), lax.axis_index("wide")
    core, x, upper = lax.rem(row, 2), lax.rem(row // 2, 4), row // 8
    y, z = wide // 8, lax.rem(wide, 8)

    def on_wide(t, dz):
        return lax.rem(y + t, 2) * 8 + lax.rem(z + dz + 8, 8)

    def on_row(t, dx, other=0):
        chip = lax.rem(upper + t, 2) * 4 + lax.rem(x + dx + 4, 4)
        return chip * 2 + (core if other == 0 else 1 - core)

    neighbours = [
        {"wide": on_wide(0, 1)}, {"wide": on_wide(0, -1)}, {"wide": on_wide(1, 0)},
        {"row": on_row(0, 1)}, {"row": on_row(0, -1)}, {"row": on_row(1, 0)}, {"row": on_row(0, 0, 1)},
    ]
    barrier = pltpu.get_barrier_semaphore()
    for where in neighbours:
        pl.semaphore_signal(barrier, inc=1, device_id=where, device_id_type=MESH)
    pl.semaphore_wait(barrier, len(neighbours))
    partner = {"row": on_row(0, 0, 1)}

    pivots = [(0, pv.at[0], gpv.at[0], 0, 0), (1, pv.at[1], gpv.at[1], 1, 0), (2, pv.at[2], gpv.at[2], 0, 1)]
    columns = [(3, cq, gcq, 0, None), (4, c7, gc7, 1, None), (5, wq, gwq, 0, None), (6, w7, gw7, 1, None)]
    rows = [(7, rq, grq, 0, None), (8, r7, gr7, 1, None)]
    sign = (1, -1)

    def only(job, f):
        if job[4] is None:
            f()
        else:
            pl.when(core == job[4])(f)

    def local(job):
        k, src, dst = job[:3]
        return pltpu.make_async_copy(src, dst.at[row if k >= 7 else wide], lsem.at[k])

    def across(job):
        k, src, dst = job[:3]
        if k >= 7:
            return remote(src, dst.at[row], xs.at[k], xr.at[k], {"row": on_row(1, 0)})
        return remote(src, dst.at[wide], xs.at[k], xr.at[k], {"wide": on_wide(1, 0)})

    def crossed(job):
        k, src, dst = job[:3]
        if k >= 7:
            return remote(src, dst.at[on_row(1, 0)], xs.at[k], xr.at[k], {"row": on_row(1, 0)})
        return remote(src, dst.at[on_wide(1, 0)], xs.at[k], xr.at[k], {"wide": on_wide(1, 0)})

    def hop(job, t, way, d, arriving=False):
        k, src, dst = job[:3]
        s = sign[way]
        back = d if arriving else d - 1
        if k >= 7:
            block = dst.at[on_row(t, -s * back)]
            start = src if isinstance(d, int) and d == 1 and t == 0 else block
            return remote(start, block, hs.at[k - 7, t, way, d], hr.at[k - 7, t, way, d], {"row": on_row(0, s)})
        block = dst.at[on_wide(t, -s * back)]
        start = src if isinstance(d, int) and d == 1 and t == 0 else block
        return remote(start, block, zs.at[k, t, way, d], zr.at[k, t, way, d], {"wide": on_wide(0, s)})

    def share(job, t, dx, arriving=False):
        k, src, dst = job[:3]
        block = dst.at[on_row(t, dx, 1 if arriving else 0)]
        rel = dx + 2
        return remote(block, block, fs.at[k - 7, t, rel], fr.at[k - 7, t, rel], partner)

    def begin(job):
        local(job).start()
        across(job).start()
        hop(job, 0, 0, 1).start()
        hop(job, 0, 1, 1).start()

    def second(job):
        crossed(job).wait_recv()
        hop(job, 1, 0, 1).start()
        hop(job, 1, 1, 1).start()

    def pass_on(job, d, ways):
        for t in (0, 1):
            for way in (0, 1):
                hop(job, t, way, d, True).wait_recv()
                if ways == 2 or (ways == 1 and way == job[3]):
                    hop(job, t, way, d + 1).start()

    def last(job, d):
        for t in (0, 1):
            hop(job, t, job[3], d, True).wait_recv()

    for job in pivots + columns + rows:
        only(job, lambda: begin(job))
    for job in pivots + columns:
        only(job, lambda: second(job))
    for job in rows:
        local(job).wait()
        share(job, 0, 0).start()
    for job in pivots + columns:
        only(job, lambda: pass_on(job, 1, 2))
    for job in rows:
        second(job)
        share(job, 1, 0).start()
    for job in pivots + columns:
        only(job, lambda: pass_on(job, 2, 2))
    for job in rows:
        pass_on(job, 1, 1)
        for t in (0, 1):
            share(job, t, -1).start()
            share(job, t, 1).start()
    for job in pivots + columns:
        only(job, lambda: pass_on(job, 3, 1))
    for job in pivots:
        def done(job=job):
            local(job).wait()
            last(job, 4)
            remote(job[2], job[2], ps.at[job[0]], pr.at[job[0]], partner).start()
        only(job, done)
    for job in rows:
        last(job, 2)
        for t in (0, 1):
            share(job, t, -2).start()
    for job in columns:
        local(job).wait()
        last(job, 4)

    def sent(job):
        across(job).wait_send()
        full = 2 if job[0] >= 7 else 4
        for t in (0, 1):
            for way in (0, 1):
                for d in range(1, full + 1 if way == job[3] else full):
                    hop(job, t, way, d).wait_send()

    for job in pivots:
        def carried(job=job):
            sent(job)
            remote(job[2], job[2], ps.at[job[0]], pr.at[job[0]], partner).wait_send()
        only(job, carried)

        @pl.when(core != job[4])
        def _():
            remote(job[2], job[2], ps.at[job[0]], pr.at[job[0]], partner).wait_recv()
    for job in columns:
        sent(job)
    for job in rows:
        sent(job)
        for t in (0, 1):
            for dx in (0, -1, 1, -2):
                share(job, t, dx, True).wait_recv()
                share(job, t, dx).wait_send()


def gather(pieces):
    outs = [piece(p.dtype, N, *p.shape) for p in PIECES[:6]] + [piece(F32, 3, N, 24, PAIR)]
    return pl.pallas_call(
        gather_kernel,
        name="gather_panels",
        out_shape=outs,
        in_specs=[ANY] * 7,
        out_specs=[ANY] * 7,
        scratch_shapes=[
            pltpu.SemaphoreType.DMA((9,)),
            pltpu.SemaphoreType.DMA((9,)),
            pltpu.SemaphoreType.DMA((9,)),
            pltpu.SemaphoreType.DMA((7, 2, 2, 5)),
            pltpu.SemaphoreType.DMA((7, 2, 2, 5)),
            pltpu.SemaphoreType.DMA((2, 2, 2, 3)),
            pltpu.SemaphoreType.DMA((2, 2, 2, 3)),
            pltpu.SemaphoreType.DMA((3,)),
            pltpu.SemaphoreType.DMA((3,)),
            pltpu.SemaphoreType.DMA((2, 2, 4)),
            pltpu.SemaphoreType.DMA((2, 2, 4)),
        ],
        compiler_params=pltpu.CompilerParams(collective_id=0, has_side_effects=True),
    )(*pieces)


def dot(a, b):
    return jnp.dot(a, b, preferred_element_type=F32)


def split(a):
    high = a.astype(BF16)
    return high, (a - high.astype(F32)).astype(BF16)


def dot3(a, b):
    ah, al = split(a)
    bh, bl = split(b)
    return dot(ah, bh) + (dot(ah, bl) + dot(al, bh))


def invert(a_ref, out_ref, s_ref, x_ref, r_ref):
    n = PAIR
    eye = (
        lax.broadcasted_iota(jnp.int32, (n, n), 0) == lax.broadcasted_iota(jnp.int32, (n, n), 1)
    ).astype(F32)
    a = a_ref[...]
    across = lax.rsqrt(jnp.sum(a * eye, axis=0, keepdims=True))
    down = lax.rsqrt(jnp.sum(a * eye, axis=1, keepdims=True))
    s = a * across * down
    s_ref[0], s_ref[1] = split(s)
    bound = jnp.max(jnp.sum(jnp.abs(s), axis=1, keepdims=True), axis=0, keepdims=True)
    start = 1.9 / bound
    x_ref[...] = start * eye
    r_ref[...] = eye - start * s

    def quick(_, c):
        r = r_ref[...].astype(BF16)
        x = x_ref[...]
        both = dot(jnp.concatenate([x.astype(BF16), r], 0), r)
        x_ref[...] = x + both[:n]
        r_ref[...] = both[n:]
        return c

    lax.fori_loop(0, 5, quick, 0)

    def careful(state):
        step, _ = state
        xh, xl = split(x_ref[...])
        r = eye - (dot(s_ref[0], xh) + (dot(s_ref[0], xl) + dot(s_ref[1], xh)))
        size = jnp.max(jnp.sum(jnp.abs(r), axis=1, keepdims=True))
        lost = jnp.logical_and(step == 0, jnp.logical_not(size < 0.9))
        near = size < 0.25
        r_ref[...] = r

        @pl.when(lost)
        def _():
            x_ref[...] = eye / bound

        @pl.when(jnp.logical_and(jnp.logical_not(lost), jnp.logical_not(near)))
        def _():
            x_ref[...] = x_ref[...] + dot3(x_ref[...], r_ref[...])

        @pl.when(near)
        def _():
            x = x_ref[...]
            x_ref[...] = x + dot(x.astype(BF16), r_ref[...].astype(BF16))

        return step + 1, jnp.where(lost, 1.0, size)

    lax.while_loop(lambda s: jnp.logical_and(s[0] < 64, s[1] > 1e-3), careful, (0, 1.0))
    out_ref[...] = x_ref[...] * across * down


def finish_kernel(other, pv, b0, b1, cq, c7, wq, w7, h, w, oh, ow,
                  s_ref, x_ref, r_ref, g_ref, c_ref, m_ref, b_ref, xh_ref, xl_ref, w_ref, sem):
    step = pl.program_id(0)
    tiles = 1152 // PAIR

    def over_tiles(f):
        def body(j, c):
            f(pl.ds(pl.multiple_of(j * PAIR, PAIR), PAIR))
            return c
        lax.fori_loop(0, tiles, body, 0)

    @pl.when(step == 0)
    def _():
        loads = [pltpu.make_async_copy(b, b_ref.at[i], sem.at[i]) for i, b in enumerate((b0, b1))]
        for load in loads:
            load.start()

        def keep(i, value):
            m_ref[i, 0], m_ref[i, 1] = split(value)

        def times(i, value):
            high, low = split(value)
            return dot(m_ref[i, 0], high) + (dot(m_ref[i, 0], low) + dot(m_ref[i, 1], high))

        invert(pv.at[0], g_ref, s_ref, x_ref, r_ref)
        keep(0, g_ref[...])
        keep(1, pv[1].T)
        t = times(0, pv[1])
        keep(3, t)
        c_ref[...] = pv[2] - times(1, t)
        invert(c_ref, g_ref, s_ref, x_ref, r_ref)
        keep(2, g_ref[...])
        for i, panel in enumerate((wq, w7)):
            for m in range(N):
                w_ref[i, 18 * m : 18 * m + 18, :] = panel[m].astype(F32)
        for load in loads:
            load.wait()

        def solve(cols):
            first = times(0, b_ref[0, :, cols])
            xb = times(2, b_ref[1, :, cols] - times(1, first))
            xa = first - times(3, xb)
            ah, al = split(xa)
            bh, bl = split(xb)
            xh_ref[0, :, cols], xl_ref[0, :, cols] = ah, al
            xh_ref[1, :, cols], xl_ref[1, :, cols] = bh, bl
            p0, p1 = w_ref[0].astype(BF16), w_ref[1].astype(BF16)
            change = (dot(p0, ah) + dot(p1, bh)) + (dot(p0, al) + dot(p1, bl))
            ow[:, cols] = (w[:, cols].astype(F32) - change).astype(BF16)

        over_tiles(solve)

    strip = h.shape[0]

    def pruned(origin, shape, dim):
        place = lax.broadcasted_iota(jnp.int32, shape, dim) + origin
        begin = other[0] * PAIR
        return jnp.logical_or(
            jnp.logical_and(place >= begin, place < begin + PAIR), place >= (NPAIRS - 1) * PAIR
        )

    lines = lax.axis_index("row") * 1152 + step * strip

    def update(j, c):
        cols = pl.ds(pl.multiple_of(j * PAIR, PAIR), PAIR)
        gone = jnp.logical_or(
            pruned(lines, (strip, PAIR), 0),
            pruned(lax.axis_index("wide") * 1152 + j * PAIR, (strip, PAIR), 1),
        )
        change = dot(cq[...], xh_ref[0, :, cols]) + dot(c7[...], xh_ref[1, :, cols])
        oh[:, cols] = jnp.where(gone, 0.0, h[:, cols] - change)
        return c

    lax.fori_loop(0, tiles, update, 0)


def finish(other, pv, b0, b1, cq, c7, wq, w7, hessian, weight):
    steps = 4
    strip = 1152 // steps

    def whole(*shape):
        return pl.BlockSpec(shape, lambda g, o: (0,) * len(shape))

    def strips(columns):
        return pl.BlockSpec((strip, columns), lambda g, o: (g, 0))

    return pl.pallas_call(
        finish_kernel,
        name="finish",
        out_shape=[piece(F32, 1152, 1152), piece(BF16, 288, 1152)],
        grid_spec=pltpu.PrefetchScalarGridSpec(
            num_scalar_prefetch=1,
            grid=(steps,),
            in_specs=[
                whole(3, PAIR, PAIR), ANY, ANY, strips(PAIR), strips(PAIR),
                whole(N, 18, PAIR), whole(N, 18, PAIR), strips(1152), whole(288, 1152),
            ],
            out_specs=[strips(1152), whole(288, 1152)],
            scratch_shapes=[
                pltpu.VMEM((2, PAIR, PAIR), BF16),
                pltpu.VMEM((PAIR, PAIR), F32),
                pltpu.VMEM((PAIR, PAIR), F32),
                pltpu.VMEM((PAIR, PAIR), F32),
                pltpu.VMEM((PAIR, PAIR), F32),
                pltpu.VMEM((4, 2, PAIR, PAIR), BF16),
                pltpu.VMEM((2, PAIR, 1152), F32),
                pltpu.VMEM((2, PAIR, 1152), BF16),
                pltpu.VMEM((2, PAIR, 1152), BF16),
                pltpu.VMEM((2, 288, PAIR), F32),
                pltpu.SemaphoreType.DMA((2,)),
            ],
        ),
    )(other, pv, b0, b1, cq, c7, wq, w7, hessian, weight)


def cut_kernel(block, hc, hr, hp, h7, wc, w7, ocq, owq, opq, orq, oc7, ow7):
    for m in range(N // 2):
        ocq[m] = hc[72 * m : 72 * m + 72, :].astype(BF16)
        oc7[m] = h7[72 * m : 72 * m + 72, :].astype(BF16)
        orq[m] = hr[24 * m : 24 * m + 24, :]
        opq[m] = hp[24 * m : 24 * m + 24, :]
    for src, out in ((wc, owq), (w7, ow7)):
        full = src[...].astype(F32)
        for m in range(N // 2):
            out[m] = full[18 * m : 18 * m + 18, :].astype(BF16)


def cut(block, hessian, weight):
    half = N // 2

    def out(*shape):
        return pl.BlockSpec((half, *shape), lambda g, b: (g, 0, 0))

    return pl.pallas_call(
        cut_kernel,
        name="cut",
        out_shape=[
            piece(BF16, N, 72, PAIR), piece(BF16, N, 18, PAIR), piece(F32, N, 24, PAIR),
            piece(F32, N, 24, 1152), piece(BF16, N, 72, PAIR), piece(BF16, N, 18, PAIR),
        ],
        grid_spec=pltpu.PrefetchScalarGridSpec(
            num_scalar_prefetch=1,
            grid=(2,),
            in_specs=[
                pl.BlockSpec((576, PAIR), lambda g, b: (g, b[0])),
                pl.BlockSpec((192, 1152), lambda g, b: (2 * b[0] + g, 0)),
                pl.BlockSpec((192, PAIR), lambda g, b: (2 * b[0] + g, b[0])),
                pl.BlockSpec((576, PAIR), lambda g, b: (g, 2)),
                pl.BlockSpec((144, PAIR), lambda g, b: (g, b[0])),
                pl.BlockSpec((144, PAIR), lambda g, b: (g, 2)),
            ],
            out_specs=[out(72, PAIR), out(18, PAIR), out(24, PAIR), out(24, 1152), out(72, PAIR), out(18, PAIR)],
        ),
    )(block, hessian, hessian, hessian, hessian, weight, weight)


def per_device(hessian, weight, pairs):
    tile = hessian.shape[0]
    per_tile = tile // PAIR
    other = jnp.minimum(pairs[0], pairs[1])
    root = other // per_tile
    block = (other % per_tile).reshape(1)
    cq, wq, pq, rq, c7, w7 = cut(block, hessian, weight)
    operands = (cq, wq, pq, rq, c7, w7, hessian)
    pieces = lax.switch(root, [functools.partial(scatter, i) for i in range(N)], *operands)
    gcq, gwq, grq, gc7, gw7, gr7, gpv = gather(pieces)

    return finish(
        other.reshape(1), gpv.reshape(3, PAIR, PAIR), grq.reshape(PAIR, tile), gr7.reshape(PAIR, tile),
        gcq.reshape(tile, PAIR), gc7.reshape(tile, PAIR), gwq, gw7, hessian, weight,
    )


def solution(mesh):
    return jax.shard_map(
        per_device,
        mesh=mesh,
        in_specs=(P("row", "wide"), P("row", "wide"), P()),
        out_specs=(P("row", "wide"), P("row", "wide")),
        check_vma=False,
    )
```

```python
import functools

import jax
import jax.numpy as jnp
from jax import lax
from jax.experimental import pallas as pl
from jax.experimental.pallas import tpu as pltpu
from jax.sharding import PartitionSpec as P

HEAD = 192
PAIR = 2 * HEAD
NPAIRS = 48
N = 16
LAST = N - 1
MESH = pl.DeviceIdType.MESH
F32 = jnp.float32
BF16 = jnp.bfloat16
ANY = pl.BlockSpec(memory_space=pl.ANY)
VM = pl.BlockSpec(memory_space=pltpu.VMEM)


def remote(src, dst, send, recv, where):
    return pltpu.make_async_remote_copy(
        src_ref=src, dst_ref=dst, send_sem=send, recv_sem=recv,
        device_id=where, device_id_type=MESH,
    )


def greet_groups():
    row, wide = lax.axis_index("row"), lax.axis_index("wide")
    barrier = pltpu.get_barrier_semaphore()

    def body(d, _):
        pl.semaphore_signal(
            barrier, inc=1, device_id={"row": lax.rem(row + d, N)}, device_id_type=MESH
        )
        pl.semaphore_signal(
            barrier, inc=1, device_id={"wide": lax.rem(wide + d, N)}, device_id_type=MESH
        )
        return 0

    lax.fori_loop(1, N, body, 0)
    pl.semaphore_wait(barrier, 2 * (N - 1))


def scatter_kernel(root, cq, wq, pq, rq, c7, w7, r7,
                   ocq, owq, orq, oc7, ow7, or7, opv, pst, ssem, rsem, lsem):
    row, wide = lax.axis_index("row"), lax.axis_index("wide")
    greet_groups()
    at_wide, at_row = wide == root, row == root
    last_wide, last_row = wide == LAST, row == LAST

    def strip(m, columns):
        return r7.at[pl.ds(pl.multiple_of(2 * PAIR + 24 * m, 8), 24), columns]

    jobs = [
        (0, jnp.logical_and(at_row, at_wide), at_row, "wide", wide, lambda m: pq.at[m], pst.at[0]),
        (1, jnp.logical_and(at_row, last_wide), at_row, "wide", wide, lambda m: rq.at[m, :, pl.ds(2 * PAIR, PAIR)], pst.at[1]),
        (2, jnp.logical_and(last_row, last_wide), last_row, "wide", wide, lambda m: strip(m, pl.ds(2 * PAIR, PAIR)), pst.at[2]),
        (3, at_row, None, "row", row, lambda m: rq.at[m], orq),
        (4, last_row, None, "row", row, lambda m: strip(m, slice(None)), or7),
        (5, at_wide, None, "wide", wide, lambda m: cq.at[m], ocq),
        (6, last_wide, None, "wide", wide, lambda m: c7.at[m], oc7),
        (7, at_wide, None, "wide", wide, lambda m: wq.at[m], owq),
        (8, last_wide, None, "wide", wide, lambda m: w7.at[m], ow7),
    ]

    def spread(job, act):
        k, mine, _, axis, me, src, dst = job

        @pl.when(mine)
        def _():
            def body(m, _):
                @pl.when(m != me)
                def _():
                    copy = remote(src(m), dst, ssem.at[k, m], rsem.at[k], {axis: m})
                    copy.start() if act == "start" else copy.wait_send()

                @pl.when(m == me)
                def _():
                    copy = pltpu.make_async_copy(src(m), dst, lsem.at[k])
                    copy.start() if act == "start" else copy.wait()
                return 0

            lax.fori_loop(0, N, body, 0)

    def arrive(job):
        k, mine, group, axis, me, src, dst = job
        away = jnp.logical_not(mine)
        if group is not None:
            away = jnp.logical_and(away, group)

        @pl.when(away)
        def _():
            remote(src(0), dst, ssem.at[k, 0], rsem.at[k], {axis: 0}).wait_recv()

    for job in jobs:
        spread(job, "start")
    for job in jobs[:3]:
        arrive(job)
        spread(job, "drain")
    second = [(9, at_row, 0, 0, root), (10, at_row, 1, 0, root), (11, last_row, 2, 1, LAST)]

    def forward(item, act):
        k, mine, part, core, origin = item

        @pl.when(mine)
        def _():
            def body(h, _):
                m = 2 * h + core

                @pl.when(m != origin)
                def _():
                    copy = remote(pst.at[part], opv.at[part], ssem.at[k, m], rsem.at[k], {"row": m})
                    copy.start() if act == "start" else copy.wait_send()

                @pl.when(m == origin)
                def _():
                    copy = pltpu.make_async_copy(pst.at[part], opv.at[part], lsem.at[k])
                    copy.start() if act == "start" else copy.wait()
                return 0

            lax.fori_loop(0, N // 2, body, 0)

    for item in second:
        forward(item, "start")
    for item in second:
        k, mine, part, core, origin = item
        away = jnp.logical_and(jnp.logical_not(mine), lax.rem(row, 2) == core)

        @pl.when(away)
        def _():
            remote(pst.at[part], opv.at[part], ssem.at[k, 0], rsem.at[k], {"row": 0}).wait_recv()

    for job in jobs[3:]:
        arrive(job)
    for item in second:
        forward(item, "drain")
    for job in jobs[3:]:
        spread(job, "drain")


def piece(dtype, *shape):
    return jax.ShapeDtypeStruct(shape, dtype)


PIECES = [
    piece(BF16, 72, PAIR), piece(BF16, 18, PAIR), piece(F32, 24, 1152),
    piece(BF16, 72, PAIR), piece(BF16, 18, PAIR), piece(F32, 24, 1152),
    piece(F32, 3, 24, PAIR),
]


def scatter(root, *operands):
    outs = PIECES + [piece(F32, 3, 24, PAIR)]
    return pl.pallas_call(
        functools.partial(scatter_kernel, root),
        name=f"scatter_{root}",
        out_shape=outs,
        in_specs=[ANY] * 7,
        out_specs=[ANY] * 8,
        scratch_shapes=[
            pltpu.SemaphoreType.DMA((12, N)),
            pltpu.SemaphoreType.DMA((12,)),
            pltpu.SemaphoreType.DMA((12,)),
        ],
        compiler_params=pltpu.CompilerParams(collective_id=1 + root, has_side_effects=True),
    )(*operands)[:7]


def gather_kernel(cq, wq, rq, c7, w7, r7, pv,
                  gcq, gwq, grq, gc7, gw7, gr7, gpv,
                  lsem, xs, xr, zs, zr, hs, hr, ps, pr, fs, fr, ys, yr):
    row, wide = lax.axis_index("row"), lax.axis_index("wide")
    core, x, upper = lax.rem(row, 2), lax.rem(row // 2, 4), row // 8
    y, z = wide // 8, lax.rem(wide, 8)

    def on_wide(t, dz):
        return lax.rem(y + t, 2) * 8 + lax.rem(z + dz + 8, 8)

    def on_row(t, dx, other=0):
        chip = lax.rem(upper + t, 2) * 4 + lax.rem(x + dx + 4, 4)
        return chip * 2 + (core if other == 0 else 1 - core)

    neighbours = [
        {"wide": on_wide(0, 1)}, {"wide": on_wide(0, -1)}, {"wide": on_wide(1, 0)},
        {"row": on_row(0, 1)}, {"row": on_row(0, -1)}, {"row": on_row(1, 0)}, {"row": on_row(0, 0, 1)},
    ]
    barrier = pltpu.get_barrier_semaphore()
    for where in neighbours:
        pl.semaphore_signal(barrier, inc=1, device_id=where, device_id_type=MESH)
    pl.semaphore_wait(barrier, len(neighbours))
    partner = {"row": on_row(0, 0, 1)}

    pivots = [(0, pv.at[0], gpv.at[0], 0, 0), (1, pv.at[1], gpv.at[1], 1, 0), (2, pv.at[2], gpv.at[2], 0, 1)]
    columns = [(3, cq, gcq, 0, None), (4, c7, gc7, 1, None), (5, wq, gwq, 0, None), (6, w7, gw7, 1, None)]
    rows = [(7, rq, grq, 0, None), (8, r7, gr7, 1, None)]
    sign = (1, -1)

    def only(job, f):
        if job[4] is None:
            f()
        else:
            pl.when(core == job[4])(f)

    def local(job):
        k, src, dst = job[:3]
        return pltpu.make_async_copy(src, dst.at[row if k >= 7 else wide], lsem.at[k])

    def across(job):
        k, src, dst = job[:3]
        if k >= 7:
            return remote(src, dst.at[row], xs.at[k], xr.at[k], {"row": on_row(1, 0)})
        return remote(src, dst.at[wide], xs.at[k], xr.at[k], {"wide": on_wide(1, 0)})

    def crossed(job):
        k, src, dst = job[:3]
        if k >= 7:
            return remote(src, dst.at[on_row(1, 0)], xs.at[k], xr.at[k], {"row": on_row(1, 0)})
        return remote(src, dst.at[on_wide(1, 0)], xs.at[k], xr.at[k], {"wide": on_wide(1, 0)})

    def hop(job, t, way, d, arriving=False):
        k, src, dst = job[:3]
        s = sign[way]
        back = d if arriving else d - 1
        if k >= 7:
            block = dst.at[on_row(t, -s * back)]
            start = src if isinstance(d, int) and d == 1 and t == 0 else block
            return remote(start, block, hs.at[k - 7, t, way, d], hr.at[k - 7, t, way, d], {"row": on_row(0, s)})
        block = dst.at[on_wide(t, -s * back)]
        start = src if isinstance(d, int) and d == 1 and t == 0 else block
        return remote(start, block, zs.at[k, t, way, d], zr.at[k, t, way, d], {"wide": on_wide(0, s)})

    def share(job, t, dx, arriving=False):
        k, src, dst = job[:3]
        block = dst.at[on_row(t, dx, 1 if arriving else 0)]
        rel = dx + 2
        return remote(block, block, fs.at[k - 7, t, rel], fr.at[k - 7, t, rel], partner)

    def sides(job):
        return (0,) if job[0] == 4 else (0, 1)

    def step_across(job, dz, arriving=False):
        block = job[2].at[on_wide(1 if arriving else 0, dz)]
        return remote(block, block, ys.at[dz + 3], yr.at[dz + 3], {"wide": on_wide(1, 0)})

    def begin(job):
        local(job).start()
        across(job).start()
        hop(job, 0, 0, 1).start()
        hop(job, 0, 1, 1).start()

    def second(job):
        if len(sides(job)) == 2:
            crossed(job).wait_recv()
            hop(job, 1, 0, 1).start()
            hop(job, 1, 1, 1).start()

    def pass_on(job, d, ways):
        for t in sides(job):
            for way in (0, 1):
                hop(job, t, way, d, True).wait_recv()
                if ways == 2 or (ways == 1 and way == job[3]):
                    hop(job, t, way, d + 1).start()
                if len(sides(job)) == 1:
                    step_across(job, -sign[way] * d).start()

    def last(job, d):
        for t in sides(job):
            hop(job, t, job[3], d, True).wait_recv()
        if len(sides(job)) == 1:
            step_across(job, -sign[job[3]] * d).start()

    for job in pivots + columns + rows:
        only(job, lambda: begin(job))
    for job in pivots + columns:
        only(job, lambda: second(job))
    for job in rows:
        local(job).wait()
        share(job, 0, 0).start()
    for job in pivots + columns:
        only(job, lambda: pass_on(job, 1, 2))
    for job in rows:
        second(job)
        share(job, 1, 0).start()
    for job in pivots + columns:
        only(job, lambda: pass_on(job, 2, 2))
    for job in rows:
        pass_on(job, 1, 1)
        for t in (0, 1):
            share(job, t, -1).start()
            share(job, t, 1).start()
    for job in pivots + columns:
        only(job, lambda: pass_on(job, 3, 1))
    for job in pivots:
        def done(job=job):
            local(job).wait()
            last(job, 4)
            remote(job[2], job[2], ps.at[job[0]], pr.at[job[0]], partner).start()
        only(job, done)
    for job in rows:
        last(job, 2)
        for t in (0, 1):
            share(job, t, -2).start()
    for job in columns:
        local(job).wait()
        last(job, 4)

    def sent(job):
        across(job).wait_send()
        full = 2 if job[0] >= 7 else 4
        if len(sides(job)) == 1:
            crossed(job).wait_recv()
            for dz in (-1, 1, -2, 2, -3, 3, 4):
                step_across(job, dz, True).wait_recv()
                step_across(job, dz).wait_send()
        for t in sides(job):
            for way in (0, 1):
                for d in range(1, full + 1 if way == job[3] else full):
                    hop(job, t, way, d).wait_send()

    for job in pivots:
        def carried(job=job):
            sent(job)
            remote(job[2], job[2], ps.at[job[0]], pr.at[job[0]], partner).wait_send()
        only(job, carried)

        @pl.when(core != job[4])
        def _():
            remote(job[2], job[2], ps.at[job[0]], pr.at[job[0]], partner).wait_recv()
    for job in columns:
        sent(job)
    for job in rows:
        sent(job)
        for t in (0, 1):
            for dx in (0, -1, 1, -2):
                share(job, t, dx, True).wait_recv()
                share(job, t, dx).wait_send()


def gather(pieces):
    outs = [piece(p.dtype, N, *p.shape) for p in PIECES[:6]] + [piece(F32, 3, N, 24, PAIR)]
    return pl.pallas_call(
        gather_kernel,
        name="gather_panels",
        out_shape=outs,
        in_specs=[ANY] * 7,
        out_specs=[ANY] * 7,
        scratch_shapes=[
            pltpu.SemaphoreType.DMA((9,)),
            pltpu.SemaphoreType.DMA((9,)),
            pltpu.SemaphoreType.DMA((9,)),
            pltpu.SemaphoreType.DMA((7, 2, 2, 5)),
            pltpu.SemaphoreType.DMA((7, 2, 2, 5)),
            pltpu.SemaphoreType.DMA((2, 2, 2, 3)),
            pltpu.SemaphoreType.DMA((2, 2, 2, 3)),
            pltpu.SemaphoreType.DMA((3,)),
            pltpu.SemaphoreType.DMA((3,)),
            pltpu.SemaphoreType.DMA((2, 2, 4)),
            pltpu.SemaphoreType.DMA((2, 2, 4)),
            pltpu.SemaphoreType.DMA((8,)),
            pltpu.SemaphoreType.DMA((8,)),
        ],
        compiler_params=pltpu.CompilerParams(collective_id=0, has_side_effects=True),
    )(*pieces)


def dot(a, b):
    return jnp.dot(a, b, preferred_element_type=F32)


def split(a):
    high = a.astype(BF16)
    return high, (a - high.astype(F32)).astype(BF16)


def dot3(a, b):
    ah, al = split(a)
    bh, bl = split(b)
    return dot(ah, bh) + (dot(ah, bl) + dot(al, bh))


def invert(a_ref, out_ref, s_ref, x_ref, r_ref):
    n = PAIR
    eye = (
        lax.broadcasted_iota(jnp.int32, (n, n), 0) == lax.broadcasted_iota(jnp.int32, (n, n), 1)
    ).astype(F32)
    a = a_ref[...]
    across = lax.rsqrt(jnp.sum(a * eye, axis=0, keepdims=True))
    down = lax.rsqrt(jnp.sum(a * eye, axis=1, keepdims=True))
    s = a * across * down
    sh, sl = split(s)
    s_ref[...] = jnp.concatenate([sh, sh, sl], 1)
    bound = jnp.max(jnp.sum(jnp.abs(s), axis=1, keepdims=True), axis=0, keepdims=True)
    start = 1.9 / bound
    x_ref[...] = start * eye
    r_ref[...] = eye - start * s

    def quick(_, c):
        r = r_ref[...].astype(BF16)
        x = x_ref[...]
        both = dot(jnp.concatenate([x.astype(BF16), r], 0), r)
        x_ref[...] = x + both[:n]
        r_ref[...] = both[n:]
        return c

    lax.fori_loop(0, 5, quick, 0)

    def careful(state):
        step, _ = state
        xh, xl = split(x_ref[...])
        r = eye - dot(s_ref[...], jnp.concatenate([xh, xl, xh], 0))
        size = jnp.max(jnp.sum(jnp.abs(r), axis=1, keepdims=True))
        lost = jnp.logical_and(step == 0, jnp.logical_not(size < 0.9))
        near = size < 0.25
        r_ref[...] = r

        @pl.when(lost)
        def _():
            x_ref[...] = eye / bound

        @pl.when(jnp.logical_and(jnp.logical_not(lost), jnp.logical_not(near)))
        def _():
            x_ref[...] = x_ref[...] + dot3(x_ref[...], r_ref[...])

        @pl.when(near)
        def _():
            x = x_ref[...]
            x_ref[...] = x + dot(x.astype(BF16), r_ref[...].astype(BF16))

        return step + 1, jnp.where(lost, 1.0, size)

    lax.while_loop(lambda s: jnp.logical_and(s[0] < 64, s[1] > 1e-3), careful, (0, 1.0))
    out_ref[...] = x_ref[...] * across * down


def finish_kernel(other, pv, b0, b1, cq, c7, wq, w7, h, w, oh, ow,
                  s_ref, x_ref, r_ref, g_ref, c_ref, m_ref, b_ref, x2_ref, w_ref, sem):
    step = pl.program_id(0)

    @pl.when(step == 0)
    def _():
        loads = [pltpu.make_async_copy(b, b_ref.at[i], sem.at[i]) for i, b in enumerate((b0, b1))]
        for load in loads:
            load.start()

        def keep(i, value):
            high, low = split(value)
            m_ref[i] = jnp.concatenate([high, high, low], 1)

        def times(i, value):
            high, low = split(value)
            return dot(m_ref[i], jnp.concatenate([high, low, high], 0))

        invert(pv.at[0], g_ref, s_ref, x_ref, r_ref)
        keep(0, g_ref[...])
        keep(1, pv[1].T)
        t = times(0, pv[1])
        keep(3, t)
        c_ref[...] = pv[2] - times(1, t)
        invert(c_ref, g_ref, s_ref, x_ref, r_ref)
        keep(2, g_ref[...])
        for i, panel in enumerate((wq, w7)):
            for m in range(N):
                w_ref[i, 18 * m : 18 * m + 18, :] = panel[m].astype(F32)
        for load in loads:
            load.wait()

        first = times(0, b_ref[0])
        xb = times(2, b_ref[1] - times(1, first))
        xa = first - times(3, xb)
        for i, part in enumerate((xa, xb)):
            high, low = split(part)
            x2_ref[i * PAIR : (i + 1) * PAIR, :] = high
            x2_ref[(i + 2) * PAIR : (i + 3) * PAIR, :] = low
        panels = [w_ref[i].astype(BF16) for i in (0, 1)]
        change = dot(jnp.concatenate(panels * 2, 1), x2_ref[...])
        ow[...] = (w[...].astype(F32) - change).astype(BF16)

    strip = h.shape[0]

    def pruned(origin, shape, dim):
        place = lax.broadcasted_iota(jnp.int32, shape, dim) + origin
        begin = other[0] * PAIR
        return jnp.logical_or(
            jnp.logical_and(place >= begin, place < begin + PAIR), place >= (NPAIRS - 1) * PAIR
        )

    lines = lax.axis_index("row") * 1152 + step * strip

    gone = jnp.logical_or(
        pruned(lines, (strip, 1152), 0), pruned(lax.axis_index("wide") * 1152, (strip, 1152), 1)
    )
    change = dot(jnp.concatenate([cq[...], c7[...]], 1), x2_ref[0 : 2 * PAIR, :])
    oh[...] = jnp.where(gone, 0.0, h[...] - change)


def finish(other, pv, b0, b1, cq, c7, wq, w7, hessian, weight):
    steps = 4
    strip = 1152 // steps

    def whole(*shape):
        return pl.BlockSpec(shape, lambda g, o: (0,) * len(shape))

    def strips(columns):
        return pl.BlockSpec((strip, columns), lambda g, o: (g, 0))

    return pl.pallas_call(
        finish_kernel,
        name="finish",
        out_shape=[piece(F32, 1152, 1152), piece(BF16, 288, 1152)],
        grid_spec=pltpu.PrefetchScalarGridSpec(
            num_scalar_prefetch=1,
            grid=(steps,),
            in_specs=[
                whole(3, PAIR, PAIR), ANY, ANY, strips(PAIR), strips(PAIR),
                whole(N, 18, PAIR), whole(N, 18, PAIR), strips(1152), whole(288, 1152),
            ],
            out_specs=[strips(1152), whole(288, 1152)],
            scratch_shapes=[
                pltpu.VMEM((PAIR, 3 * PAIR), BF16),
                pltpu.VMEM((PAIR, PAIR), F32),
                pltpu.VMEM((PAIR, PAIR), F32),
                pltpu.VMEM((PAIR, PAIR), F32),
                pltpu.VMEM((PAIR, PAIR), F32),
                pltpu.VMEM((4, PAIR, 3 * PAIR), BF16),
                pltpu.VMEM((2, PAIR, 1152), F32),
                pltpu.VMEM((4 * PAIR, 1152), BF16),
                pltpu.VMEM((2, 288, PAIR), F32),
                pltpu.SemaphoreType.DMA((2,)),
            ],
        ),
    )(other, pv, b0, b1, cq, c7, wq, w7, hessian, weight)


def cut_kernel(block, hc, hr, hp, h7, wc, w7, ocq, owq, opq, orq, oc7, ow7):
    for m in range(N // 2):
        ocq[m] = hc[72 * m : 72 * m + 72, :].astype(BF16)
        oc7[m] = h7[72 * m : 72 * m + 72, :].astype(BF16)
        orq[m] = hr[24 * m : 24 * m + 24, :]
        opq[m] = hp[24 * m : 24 * m + 24, :]
    for src, out in ((wc, owq), (w7, ow7)):
        full = src[...].astype(F32)
        for m in range(N // 2):
            out[m] = full[18 * m : 18 * m + 18, :].astype(BF16)


def cut(block, hessian, weight):
    half = N // 2

    def out(*shape):
        return pl.BlockSpec((half, *shape), lambda g, b: (g, 0, 0))

    return pl.pallas_call(
        cut_kernel,
        name="cut",
        out_shape=[
            piece(BF16, N, 72, PAIR), piece(BF16, N, 18, PAIR), piece(F32, N, 24, PAIR),
            piece(F32, N, 24, 1152), piece(BF16, N, 72, PAIR), piece(BF16, N, 18, PAIR),
        ],
        grid_spec=pltpu.PrefetchScalarGridSpec(
            num_scalar_prefetch=1,
            grid=(2,),
            in_specs=[
                pl.BlockSpec((576, PAIR), lambda g, b: (g, b[0])),
                pl.BlockSpec((192, 1152), lambda g, b: (2 * b[0] + g, 0)),
                pl.BlockSpec((192, PAIR), lambda g, b: (2 * b[0] + g, b[0])),
                pl.BlockSpec((576, PAIR), lambda g, b: (g, 2)),
                pl.BlockSpec((144, PAIR), lambda g, b: (g, b[0])),
                pl.BlockSpec((144, PAIR), lambda g, b: (g, 2)),
            ],
            out_specs=[out(72, PAIR), out(18, PAIR), out(24, PAIR), out(24, 1152), out(72, PAIR), out(18, PAIR)],
        ),
    )(block, hessian, hessian, hessian, hessian, weight, weight)


def per_device(hessian, weight, pairs):
    tile = hessian.shape[0]
    per_tile = tile // PAIR
    other = jnp.minimum(pairs[0], pairs[1])
    root = other // per_tile
    block = (other % per_tile).reshape(1)
    cq, wq, pq, rq, c7, w7 = cut(block, hessian, weight)
    operands = (cq, wq, pq, rq, c7, w7, hessian)
    pieces = lax.switch(root, [functools.partial(scatter, i) for i in range(N)], *operands)
    gcq, gwq, grq, gc7, gw7, gr7, gpv = gather(pieces)

    return finish(
        other.reshape(1), gpv.reshape(3, PAIR, PAIR), grq.reshape(PAIR, tile), gr7.reshape(PAIR, tile),
        gcq.reshape(tile, PAIR), gc7.reshape(tile, PAIR), gwq, gw7, hessian, weight,
    )


def solution(mesh):
    return jax.shard_map(
        per_device,
        mesh=mesh,
        in_specs=(P("row", "wide"), P("row", "wide"), P()),
        out_specs=(P("row", "wide"), P("row", "wide")),
        check_vma=False,
    )
```

```python
import functools

import jax
import jax.numpy as jnp
from jax import lax
from jax.experimental import pallas as pl
from jax.experimental.pallas import tpu as pltpu
from jax.sharding import PartitionSpec as P

HEAD = 192
PAIR = 2 * HEAD
NPAIRS = 48
N = 16
LAST = N - 1
MESH = pl.DeviceIdType.MESH
F32 = jnp.float32
BF16 = jnp.bfloat16
ANY = pl.BlockSpec(memory_space=pl.ANY)
VM = pl.BlockSpec(memory_space=pltpu.VMEM)


def remote(src, dst, send, recv, where):
    return pltpu.make_async_remote_copy(
        src_ref=src, dst_ref=dst, send_sem=send, recv_sem=recv,
        device_id=where, device_id_type=MESH,
    )


def greet_groups():
    row, wide = lax.axis_index("row"), lax.axis_index("wide")
    barrier = pltpu.get_barrier_semaphore()

    def body(d, _):
        pl.semaphore_signal(
            barrier, inc=1, device_id={"row": lax.rem(row + d, N)}, device_id_type=MESH
        )
        pl.semaphore_signal(
            barrier, inc=1, device_id={"wide": lax.rem(wide + d, N)}, device_id_type=MESH
        )
        return 0

    lax.fori_loop(1, N, body, 0)
    pl.semaphore_wait(barrier, 2 * (N - 1))


def scatter_kernel(root, cq, wq, pq, rq, c7, w7, r7,
                   ocq, owq, orq, oc7, ow7, or7, opv, pst, ssem, rsem, lsem):
    row, wide = lax.axis_index("row"), lax.axis_index("wide")
    greet_groups()
    at_wide, at_row = wide == root, row == root
    last_wide, last_row = wide == LAST, row == LAST

    def strip(m, columns):
        return r7.at[pl.ds(pl.multiple_of(2 * PAIR + 24 * m, 8), 24), columns]

    jobs = [
        (0, jnp.logical_and(at_row, at_wide), at_row, "wide", wide, lambda m: pq.at[m], pst.at[0]),
        (1, jnp.logical_and(at_row, last_wide), at_row, "wide", wide, lambda m: rq.at[m, :, pl.ds(2 * PAIR, PAIR)], pst.at[1]),
        (2, jnp.logical_and(last_row, last_wide), last_row, "wide", wide, lambda m: strip(m, pl.ds(2 * PAIR, PAIR)), pst.at[2]),
        (3, at_row, None, "row", row, lambda m: rq.at[m], orq),
        (4, last_row, None, "row", row, lambda m: strip(m, slice(None)), or7),
        (5, at_wide, None, "wide", wide, lambda m: cq.at[m], ocq),
        (6, last_wide, None, "wide", wide, lambda m: c7.at[m], oc7),
        (7, at_wide, None, "wide", wide, lambda m: wq.at[m], owq),
        (8, last_wide, None, "wide", wide, lambda m: w7.at[m], ow7),
    ]

    def spread(job, act):
        k, mine, _, axis, me, src, dst = job

        @pl.when(mine)
        def _():
            def body(m, _):
                @pl.when(m != me)
                def _():
                    copy = remote(src(m), dst, ssem.at[k, m], rsem.at[k], {axis: m})
                    copy.start() if act == "start" else copy.wait_send()

                @pl.when(m == me)
                def _():
                    copy = pltpu.make_async_copy(src(m), dst, lsem.at[k])
                    copy.start() if act == "start" else copy.wait()
                return 0

            lax.fori_loop(0, N, body, 0)

    def arrive(job):
        k, mine, group, axis, me, src, dst = job
        away = jnp.logical_not(mine)
        if group is not None:
            away = jnp.logical_and(away, group)

        @pl.when(away)
        def _():
            remote(src(0), dst, ssem.at[k, 0], rsem.at[k], {axis: 0}).wait_recv()

    for job in jobs:
        spread(job, "start")
    for job in jobs[:3]:
        arrive(job)
        spread(job, "drain")
    second = [(9, at_row, 0, 0, root), (10, at_row, 1, 0, root), (11, last_row, 2, 1, LAST)]

    def forward(item, act):
        k, mine, part, core, origin = item

        @pl.when(mine)
        def _():
            def body(h, _):
                m = 2 * h + core

                @pl.when(m != origin)
                def _():
                    copy = remote(pst.at[part], opv.at[part], ssem.at[k, m], rsem.at[k], {"row": m})
                    copy.start() if act == "start" else copy.wait_send()

                @pl.when(m == origin)
                def _():
                    copy = pltpu.make_async_copy(pst.at[part], opv.at[part], lsem.at[k])
                    copy.start() if act == "start" else copy.wait()
                return 0

            lax.fori_loop(0, N // 2, body, 0)

    for item in second:
        forward(item, "start")
    for item in second:
        k, mine, part, core, origin = item
        away = jnp.logical_and(jnp.logical_not(mine), lax.rem(row, 2) == core)

        @pl.when(away)
        def _():
            remote(pst.at[part], opv.at[part], ssem.at[k, 0], rsem.at[k], {"row": 0}).wait_recv()

    for job in jobs[3:]:
        arrive(job)
    for item in second:
        forward(item, "drain")
    for job in jobs[3:]:
        spread(job, "drain")


def piece(dtype, *shape):
    return jax.ShapeDtypeStruct(shape, dtype)


PIECES = [
    piece(BF16, 72, PAIR), piece(BF16, 18, PAIR), piece(F32, 24, 1152),
    piece(BF16, 72, PAIR), piece(BF16, 18, PAIR), piece(F32, 24, 1152),
    piece(F32, 3, 24, PAIR),
]


def scatter(root, *operands):
    outs = PIECES + [piece(F32, 3, 24, PAIR)]
    return pl.pallas_call(
        functools.partial(scatter_kernel, root),
        name=f"scatter_{root}",
        out_shape=outs,
        in_specs=[ANY] * 7,
        out_specs=[ANY] * 8,
        scratch_shapes=[
            pltpu.SemaphoreType.DMA((12, N)),
            pltpu.SemaphoreType.DMA((12,)),
            pltpu.SemaphoreType.DMA((12,)),
        ],
        compiler_params=pltpu.CompilerParams(collective_id=1 + root, has_side_effects=True),
    )(*operands)[:7]


def gather_kernel(cq, wq, rq, c7, w7, r7, pv,
                  gcq, gwq, grq, gc7, gw7, gr7, gpv,
                  lsem, xs, xr, zs, zr, hs, hr, ps, pr, fs, fr, ys, yr):
    row, wide = lax.axis_index("row"), lax.axis_index("wide")
    core, x, upper = lax.rem(row, 2), lax.rem(row // 2, 4), row // 8
    y, z = wide // 8, lax.rem(wide, 8)

    def on_wide(t, dz):
        return lax.rem(y + t, 2) * 8 + lax.rem(z + dz + 8, 8)

    def on_row(t, dx, other=0):
        chip = lax.rem(upper + t, 2) * 4 + lax.rem(x + dx + 4, 4)
        return chip * 2 + (core if other == 0 else 1 - core)

    neighbours = [
        {"wide": on_wide(0, 1)}, {"wide": on_wide(0, -1)}, {"wide": on_wide(1, 0)},
        {"row": on_row(0, 1)}, {"row": on_row(0, -1)}, {"row": on_row(1, 0)}, {"row": on_row(0, 0, 1)},
    ]
    barrier = pltpu.get_barrier_semaphore()
    for where in neighbours:
        pl.semaphore_signal(barrier, inc=1, device_id=where, device_id_type=MESH)
    pl.semaphore_wait(barrier, len(neighbours))
    partner = {"row": on_row(0, 0, 1)}

    pivots = [(0, pv.at[0], gpv.at[0], 0, 0), (1, pv.at[1], gpv.at[1], 1, 0), (2, pv.at[2], gpv.at[2], 0, 1)]
    columns = [(3, cq, gcq, 0, None), (4, c7, gc7, 1, None), (5, wq, gwq, 0, None), (6, w7, gw7, 1, None)]
    rows = [(7, rq, grq, 0, None), (8, r7, gr7, 1, None)]
    sign = (1, -1)

    def only(job, f):
        if job[4] is None:
            f()
        else:
            pl.when(core == job[4])(f)

    def local(job):
        k, src, dst = job[:3]
        return pltpu.make_async_copy(src, dst.at[row if k >= 7 else wide], lsem.at[k])

    def across(job):
        k, src, dst = job[:3]
        if k >= 7:
            return remote(src, dst.at[row], xs.at[k], xr.at[k], {"row": on_row(1, 0)})
        return remote(src, dst.at[wide], xs.at[k], xr.at[k], {"wide": on_wide(1, 0)})

    def crossed(job):
        k, src, dst = job[:3]
        if k >= 7:
            return remote(src, dst.at[on_row(1, 0)], xs.at[k], xr.at[k], {"row": on_row(1, 0)})
        return remote(src, dst.at[on_wide(1, 0)], xs.at[k], xr.at[k], {"wide": on_wide(1, 0)})

    def hop(job, t, way, d, arriving=False):
        k, src, dst = job[:3]
        s = sign[way]
        back = d if arriving else d - 1
        if k >= 7:
            block = dst.at[on_row(t, -s * back)]
            start = src if isinstance(d, int) and d == 1 and t == 0 else block
            return remote(start, block, hs.at[k - 7, t, way, d], hr.at[k - 7, t, way, d], {"row": on_row(0, s)})
        block = dst.at[on_wide(t, -s * back)]
        start = src if isinstance(d, int) and d == 1 and t == 0 else block
        return remote(start, block, zs.at[k, t, way, d], zr.at[k, t, way, d], {"wide": on_wide(0, s)})

    def share(job, t, dx, arriving=False):
        k, src, dst = job[:3]
        block = dst.at[on_row(t, dx, 1 if arriving else 0)]
        rel = dx + 2
        return remote(block, block, fs.at[k - 7, t, rel], fr.at[k - 7, t, rel], partner)

    def sides(job):
        return (0,) if job[0] == 4 else (0, 1)

    def step_across(job, dz, arriving=False):
        block = job[2].at[on_wide(1 if arriving else 0, dz)]
        return remote(block, block, ys.at[dz + 3], yr.at[dz + 3], {"wide": on_wide(1, 0)})

    def begin(job):
        local(job).start()
        across(job).start()
        hop(job, 0, 0, 1).start()
        hop(job, 0, 1, 1).start()

    def second(job):
        if len(sides(job)) == 2:
            crossed(job).wait_recv()
            hop(job, 1, 0, 1).start()
            hop(job, 1, 1, 1).start()

    def pass_on(job, d, ways):
        for t in sides(job):
            for way in (0, 1):
                hop(job, t, way, d, True).wait_recv()
                if ways == 2 or (ways == 1 and way == job[3]):
                    hop(job, t, way, d + 1).start()
                if len(sides(job)) == 1:
                    step_across(job, -sign[way] * d).start()

    def last(job, d):
        for t in sides(job):
            hop(job, t, job[3], d, True).wait_recv()
        if len(sides(job)) == 1:
            step_across(job, -sign[job[3]] * d).start()

    def pass_row(job, t):
        for way in (0, 1):
            hop(job, t, way, 1, True).wait_recv()
            if way == job[3]:
                hop(job, t, way, 2).start()
            share(job, t, -sign[way]).start()

    def last_row(job, t):
        hop(job, t, job[3], 2, True).wait_recv()
        share(job, t, -2).start()

    for job in pivots + columns:
        only(job, lambda: begin(job))
    for job in rows:
        local(job).start()
        hop(job, 0, 0, 1).start()
        hop(job, 0, 1, 1).start()
    for job in pivots + columns:
        only(job, lambda: second(job))
    for job in rows:
        across(job).start()
    for job in rows:
        local(job).wait()
        share(job, 0, 0).start()
    for job in pivots + columns:
        only(job, lambda: pass_on(job, 1, 2))
    for job in rows:
        pass_row(job, 0)
    for job in pivots + columns:
        only(job, lambda: pass_on(job, 2, 2))
    for job in rows:
        second(job)
        share(job, 1, 0).start()
    for job in pivots + columns:
        only(job, lambda: pass_on(job, 3, 1))
    for job in rows:
        pass_row(job, 1)
        last_row(job, 0)
    for job in pivots:
        def done(job=job):
            local(job).wait()
            last(job, 4)
            remote(job[2], job[2], ps.at[job[0]], pr.at[job[0]], partner).start()
        only(job, done)
    for job in columns:
        local(job).wait()
        last(job, 4)
    for job in rows:
        last_row(job, 1)

    def sent(job):
        across(job).wait_send()
        full = 2 if job[0] >= 7 else 4
        if len(sides(job)) == 1:
            crossed(job).wait_recv()
            for dz in (-1, 1, -2, 2, -3, 3, 4):
                step_across(job, dz, True).wait_recv()
                step_across(job, dz).wait_send()
        for t in sides(job):
            for way in (0, 1):
                for d in range(1, full + 1 if way == job[3] else full):
                    hop(job, t, way, d).wait_send()

    for job in pivots:
        def carried(job=job):
            sent(job)
            remote(job[2], job[2], ps.at[job[0]], pr.at[job[0]], partner).wait_send()
        only(job, carried)

        @pl.when(core != job[4])
        def _():
            remote(job[2], job[2], ps.at[job[0]], pr.at[job[0]], partner).wait_recv()
    for job in columns:
        sent(job)
    for job in rows:
        sent(job)
        for t in (0, 1):
            for dx in (0, -1, 1, -2):
                share(job, t, dx, True).wait_recv()
                share(job, t, dx).wait_send()


def gather(pieces):
    outs = [piece(p.dtype, N, *p.shape) for p in PIECES[:6]] + [piece(F32, 3, N, 24, PAIR)]
    return pl.pallas_call(
        gather_kernel,
        name="gather_panels",
        out_shape=outs,
        in_specs=[ANY] * 7,
        out_specs=[ANY] * 7,
        scratch_shapes=[
            pltpu.SemaphoreType.DMA((9,)),
            pltpu.SemaphoreType.DMA((9,)),
            pltpu.SemaphoreType.DMA((9,)),
            pltpu.SemaphoreType.DMA((7, 2, 2, 5)),
            pltpu.SemaphoreType.DMA((7, 2, 2, 5)),
            pltpu.SemaphoreType.DMA((2, 2, 2, 3)),
            pltpu.SemaphoreType.DMA((2, 2, 2, 3)),
            pltpu.SemaphoreType.DMA((3,)),
            pltpu.SemaphoreType.DMA((3,)),
            pltpu.SemaphoreType.DMA((2, 2, 4)),
            pltpu.SemaphoreType.DMA((2, 2, 4)),
            pltpu.SemaphoreType.DMA((8,)),
            pltpu.SemaphoreType.DMA((8,)),
        ],
        compiler_params=pltpu.CompilerParams(collective_id=0, has_side_effects=True),
    )(*pieces)


def dot(a, b):
    return jnp.dot(a, b, preferred_element_type=F32)


def split(a):
    high = a.astype(BF16)
    return high, (a - high.astype(F32)).astype(BF16)


def dot3(a, b):
    ah, al = split(a)
    bh, bl = split(b)
    return dot(ah, bh) + (dot(ah, bl) + dot(al, bh))


def invert(a_ref, out_ref, s_ref, x_ref, r_ref):
    n = PAIR
    eye = (
        lax.broadcasted_iota(jnp.int32, (n, n), 0) == lax.broadcasted_iota(jnp.int32, (n, n), 1)
    ).astype(F32)
    a = a_ref[...]
    across = lax.rsqrt(jnp.sum(a * eye, axis=0, keepdims=True))
    down = lax.rsqrt(jnp.sum(a * eye, axis=1, keepdims=True))
    s = a * across * down
    sh, sl = split(s)
    s_ref[...] = jnp.concatenate([sh, sh, sl], 1)
    bound = jnp.max(jnp.sum(jnp.abs(s), axis=1, keepdims=True), axis=0, keepdims=True)
    start = 1.9 / bound
    x_ref[...] = start * eye
    r_ref[...] = eye - start * s

    def quick(_, c):
        r = r_ref[...].astype(BF16)
        x = x_ref[...]
        both = dot(jnp.concatenate([x.astype(BF16), r], 0), r)
        x_ref[...] = x + both[:n]
        r_ref[...] = both[n:]
        return c

    lax.fori_loop(0, 4, quick, 0)

    def careful(state):
        step, _ = state
        xh, xl = split(x_ref[...])
        r = eye - dot(s_ref[...], jnp.concatenate([xh, xl, xh], 0))
        size = jnp.max(jnp.sum(jnp.abs(r), axis=1, keepdims=True))
        lost = jnp.logical_and(step == 0, jnp.logical_not(size < 0.9))
        near = size < 0.25
        r_ref[...] = r

        @pl.when(lost)
        def _():
            x_ref[...] = eye / bound

        @pl.when(jnp.logical_and(jnp.logical_not(lost), jnp.logical_not(near)))
        def _():
            x_ref[...] = x_ref[...] + dot3(x_ref[...], r_ref[...])

        @pl.when(near)
        def _():
            x = x_ref[...]
            x_ref[...] = x + dot(x.astype(BF16), r_ref[...].astype(BF16))

        return step + 1, jnp.where(lost, 1.0, size)

    lax.while_loop(lambda s: jnp.logical_and(s[0] < 64, s[1] > 1e-3), careful, (0, 1.0))
    out_ref[...] = x_ref[...] * across * down


def finish_kernel(other, pv, b0, b1, cq, c7, wq, w7, h, w, oh, ow,
                  s_ref, x_ref, r_ref, g_ref, c_ref, m_ref, b_ref, x2_ref, w_ref, sem):
    step = pl.program_id(0)

    @pl.when(step == 0)
    def _():
        loads = [pltpu.make_async_copy(b, b_ref.at[i], sem.at[i]) for i, b in enumerate((b0, b1))]
        for load in loads:
            load.start()

        def keep(i, value):
            high, low = split(value)
            m_ref[i] = jnp.concatenate([high, high, low], 1)

        def times(i, value):
            high, low = split(value)
            return dot(m_ref[i], jnp.concatenate([high, low, high], 0))

        invert(pv.at[0], g_ref, s_ref, x_ref, r_ref)
        keep(0, g_ref[...])
        keep(1, pv[1].T)
        t = times(0, pv[1])
        keep(3, t)
        c_ref[...] = pv[2] - times(1, t)
        invert(c_ref, g_ref, s_ref, x_ref, r_ref)
        keep(2, g_ref[...])
        for i, panel in enumerate((wq, w7)):
            for m in range(N):
                w_ref[i, 18 * m : 18 * m + 18, :] = panel[m].astype(F32)
        for load in loads:
            load.wait()

        first = times(0, b_ref[0])
        xb = times(2, b_ref[1] - times(1, first))
        xa = first - times(3, xb)
        for i, part in enumerate((xa, xb)):
            high, low = split(part)
            x2_ref[i * PAIR : (i + 1) * PAIR, :] = high
            x2_ref[(i + 2) * PAIR : (i + 3) * PAIR, :] = low
        panels = [w_ref[i].astype(BF16) for i in (0, 1)]
        change = dot(jnp.concatenate(panels * 2, 1), x2_ref[...])
        ow[...] = (w[...].astype(F32) - change).astype(BF16)

    strip = h.shape[0]

    def pruned(origin, shape, dim):
        place = lax.broadcasted_iota(jnp.int32, shape, dim) + origin
        begin = other[0] * PAIR
        return jnp.logical_or(
            jnp.logical_and(place >= begin, place < begin + PAIR), place >= (NPAIRS - 1) * PAIR
        )

    lines = lax.axis_index("row") * 1152 + step * strip

    gone = jnp.logical_or(
        pruned(lines, (strip, 1152), 0), pruned(lax.axis_index("wide") * 1152, (strip, 1152), 1)
    )
    change = dot(jnp.concatenate([cq[...], c7[...]], 1), x2_ref[0 : 2 * PAIR, :])
    oh[...] = jnp.where(gone, 0.0, h[...] - change)


def finish(other, pv, b0, b1, cq, c7, wq, w7, hessian, weight):
    steps = 4
    strip = 1152 // steps

    def whole(*shape):
        return pl.BlockSpec(shape, lambda g, o: (0,) * len(shape))

    def strips(columns):
        return pl.BlockSpec((strip, columns), lambda g, o: (g, 0))

    return pl.pallas_call(
        finish_kernel,
        name="finish",
        out_shape=[piece(F32, 1152, 1152), piece(BF16, 288, 1152)],
        grid_spec=pltpu.PrefetchScalarGridSpec(
            num_scalar_prefetch=1,
            grid=(steps,),
            in_specs=[
                whole(3, PAIR, PAIR), ANY, ANY, strips(PAIR), strips(PAIR),
                whole(N, 18, PAIR), whole(N, 18, PAIR), strips(1152), whole(288, 1152),
            ],
            out_specs=[strips(1152), whole(288, 1152)],
            scratch_shapes=[
                pltpu.VMEM((PAIR, 3 * PAIR), BF16),
                pltpu.VMEM((PAIR, PAIR), F32),
                pltpu.VMEM((PAIR, PAIR), F32),
                pltpu.VMEM((PAIR, PAIR), F32),
                pltpu.VMEM((PAIR, PAIR), F32),
                pltpu.VMEM((4, PAIR, 3 * PAIR), BF16),
                pltpu.VMEM((2, PAIR, 1152), F32),
                pltpu.VMEM((4 * PAIR, 1152), BF16),
                pltpu.VMEM((2, 288, PAIR), F32),
                pltpu.SemaphoreType.DMA((2,)),
            ],
        ),
    )(other, pv, b0, b1, cq, c7, wq, w7, hessian, weight)


def cut_kernel(block, hc, hr, hp, h7, wc, w7, ocq, owq, opq, orq, oc7, ow7):
    for m in range(N // 2):
        ocq[m] = hc[72 * m : 72 * m + 72, :].astype(BF16)
        oc7[m] = h7[72 * m : 72 * m + 72, :].astype(BF16)
        orq[m] = hr[24 * m : 24 * m + 24, :]
        opq[m] = hp[24 * m : 24 * m + 24, :]
    for src, out in ((wc, owq), (w7, ow7)):
        full = src[...].astype(F32)
        for m in range(N // 2):
            out[m] = full[18 * m : 18 * m + 18, :].astype(BF16)


def cut(block, hessian, weight):
    half = N // 2

    def out(*shape):
        return pl.BlockSpec((half, *shape), lambda g, b: (g, 0, 0))

    return pl.pallas_call(
        cut_kernel,
        name="cut",
        out_shape=[
            piece(BF16, N, 72, PAIR), piece(BF16, N, 18, PAIR), piece(F32, N, 24, PAIR),
            piece(F32, N, 24, 1152), piece(BF16, N, 72, PAIR), piece(BF16, N, 18, PAIR),
        ],
        grid_spec=pltpu.PrefetchScalarGridSpec(
            num_scalar_prefetch=1,
            grid=(2,),
            in_specs=[
                pl.BlockSpec((576, PAIR), lambda g, b: (g, b[0])),
                pl.BlockSpec((192, 1152), lambda g, b: (2 * b[0] + g, 0)),
                pl.BlockSpec((192, PAIR), lambda g, b: (2 * b[0] + g, b[0])),
                pl.BlockSpec((576, PAIR), lambda g, b: (g, 2)),
                pl.BlockSpec((144, PAIR), lambda g, b: (g, b[0])),
                pl.BlockSpec((144, PAIR), lambda g, b: (g, 2)),
            ],
            out_specs=[out(72, PAIR), out(18, PAIR), out(24, PAIR), out(24, 1152), out(72, PAIR), out(18, PAIR)],
        ),
    )(block, hessian, hessian, hessian, hessian, weight, weight)


def per_device(hessian, weight, pairs):
    tile = hessian.shape[0]
    per_tile = tile // PAIR
    other = jnp.minimum(pairs[0], pairs[1])
    root = other // per_tile
    block = (other % per_tile).reshape(1)
    cq, wq, pq, rq, c7, w7 = cut(block, hessian, weight)
    operands = (cq, wq, pq, rq, c7, w7, hessian)
    pieces = lax.switch(root, [functools.partial(scatter, i) for i in range(N)], *operands)
    gcq, gwq, grq, gc7, gw7, gr7, gpv = gather(pieces)

    return finish(
        other.reshape(1), gpv.reshape(3, PAIR, PAIR), grq.reshape(PAIR, tile), gr7.reshape(PAIR, tile),
        gcq.reshape(tile, PAIR), gc7.reshape(tile, PAIR), gwq, gw7, hessian, weight,
    )


def solution(mesh):
    return jax.shard_map(
        per_device,
        mesh=mesh,
        in_specs=(P("row", "wide"), P("row", "wide"), P()),
        out_specs=(P("row", "wide"), P("row", "wide")),
        check_vma=False,
    )
```

```python
import functools

import jax
import jax.numpy as jnp
from jax import lax
from jax.experimental import pallas as pl
from jax.experimental.pallas import tpu as pltpu
from jax.sharding import PartitionSpec as P

HEAD = 192
PAIR = 2 * HEAD
NPAIRS = 48
N = 16
LAST = N - 1
MESH = pl.DeviceIdType.MESH
F32 = jnp.float32
BF16 = jnp.bfloat16
ANY = pl.BlockSpec(memory_space=pl.ANY)
VM = pl.BlockSpec(memory_space=pltpu.VMEM)


def remote(src, dst, send, recv, where):
    return pltpu.make_async_remote_copy(
        src_ref=src, dst_ref=dst, send_sem=send, recv_sem=recv,
        device_id=where, device_id_type=MESH,
    )


def greet_groups():
    row, wide = lax.axis_index("row"), lax.axis_index("wide")
    barrier = pltpu.get_barrier_semaphore()

    def body(d, _):
        pl.semaphore_signal(
            barrier, inc=1, device_id={"row": lax.rem(row + d, N)}, device_id_type=MESH
        )
        pl.semaphore_signal(
            barrier, inc=1, device_id={"wide": lax.rem(wide + d, N)}, device_id_type=MESH
        )
        return 0

    lax.fori_loop(1, N, body, 0)
    pl.semaphore_wait(barrier, 2 * (N - 1))


def scatter_kernel(root, cq, wq, pq, rq, c7, w7, r7,
                   ocq, owq, orq, oc7, ow7, or7, opv, pst, ssem, rsem, lsem):
    row, wide = lax.axis_index("row"), lax.axis_index("wide")
    greet_groups()
    at_wide, at_row = wide == root, row == root
    last_wide, last_row = wide == LAST, row == LAST

    def strip(m, columns):
        return r7.at[pl.ds(pl.multiple_of(2 * PAIR + 24 * m, 8), 24), columns]

    jobs = [
        (0, jnp.logical_and(at_row, at_wide), at_row, "wide", wide, lambda m: pq.at[m], pst.at[0]),
        (1, jnp.logical_and(at_row, last_wide), at_row, "wide", wide, lambda m: rq.at[m, :, pl.ds(2 * PAIR, PAIR)], pst.at[1]),
        (2, jnp.logical_and(last_row, last_wide), last_row, "wide", wide, lambda m: strip(m, pl.ds(2 * PAIR, PAIR)), pst.at[2]),
        (3, at_row, None, "row", row, lambda m: rq.at[m], orq),
        (4, last_row, None, "row", row, lambda m: strip(m, slice(None)), or7),
        (5, at_wide, None, "wide", wide, lambda m: cq.at[m], ocq),
        (6, last_wide, None, "wide", wide, lambda m: c7.at[m], oc7),
        (7, at_wide, None, "wide", wide, lambda m: wq.at[m], owq),
        (8, last_wide, None, "wide", wide, lambda m: w7.at[m], ow7),
    ]

    def spread(job, act):
        k, mine, _, axis, me, src, dst = job

        @pl.when(mine)
        def _():
            def body(m, _):
                @pl.when(m != me)
                def _():
                    copy = remote(src(m), dst, ssem.at[k, m], rsem.at[k], {axis: m})
                    copy.start() if act == "start" else copy.wait_send()

                @pl.when(m == me)
                def _():
                    copy = pltpu.make_async_copy(src(m), dst, lsem.at[k])
                    copy.start() if act == "start" else copy.wait()
                return 0

            lax.fori_loop(0, N, body, 0)

    def arrive(job):
        k, mine, group, axis, me, src, dst = job
        away = jnp.logical_not(mine)
        if group is not None:
            away = jnp.logical_and(away, group)

        @pl.when(away)
        def _():
            remote(src(0), dst, ssem.at[k, 0], rsem.at[k], {axis: 0}).wait_recv()

    for job in jobs:
        spread(job, "start")
    for job in jobs[:3]:
        arrive(job)
        spread(job, "drain")
    second = [(9, at_row, 0, 0, root), (10, at_row, 1, 0, root), (11, last_row, 2, 1, LAST)]

    def forward(item, act):
        k, mine, part, core, origin = item

        @pl.when(mine)
        def _():
            def body(h, _):
                m = 2 * h + core

                @pl.when(m != origin)
                def _():
                    copy = remote(pst.at[part], opv.at[part], ssem.at[k, m], rsem.at[k], {"row": m})
                    copy.start() if act == "start" else copy.wait_send()

                @pl.when(m == origin)
                def _():
                    copy = pltpu.make_async_copy(pst.at[part], opv.at[part], lsem.at[k])
                    copy.start() if act == "start" else copy.wait()
                return 0

            lax.fori_loop(0, N // 2, body, 0)

    for item in second:
        forward(item, "start")
    for item in second:
        k, mine, part, core, origin = item
        away = jnp.logical_and(jnp.logical_not(mine), lax.rem(row, 2) == core)

        @pl.when(away)
        def _():
            remote(pst.at[part], opv.at[part], ssem.at[k, 0], rsem.at[k], {"row": 0}).wait_recv()

    for job in jobs[3:]:
        arrive(job)
    for item in second:
        forward(item, "drain")
    for job in jobs[3:]:
        spread(job, "drain")


def piece(dtype, *shape):
    return jax.ShapeDtypeStruct(shape, dtype)


PIECES = [
    piece(BF16, 72, PAIR), piece(BF16, 18, PAIR), piece(F32, 24, 1152),
    piece(BF16, 72, PAIR), piece(BF16, 18, PAIR), piece(F32, 24, 1152),
    piece(F32, 3, 24, PAIR),
]


def scatter(root, *operands):
    outs = PIECES + [piece(F32, 3, 24, PAIR)]
    return pl.pallas_call(
        functools.partial(scatter_kernel, root),
        name=f"scatter_{root}",
        out_shape=outs,
        in_specs=[ANY] * 7,
        out_specs=[ANY] * 8,
        scratch_shapes=[
            pltpu.SemaphoreType.DMA((12, N)),
            pltpu.SemaphoreType.DMA((12,)),
            pltpu.SemaphoreType.DMA((12,)),
        ],
        compiler_params=pltpu.CompilerParams(collective_id=1 + root, has_side_effects=True),
    )(*operands)[:7]


def gather_kernel(cq, wq, rq, c7, w7, r7, pv,
                  gcq, gwq, grq, gc7, gw7, gr7, gpv,
                  lsem, xs, xr, zs, zr, hs, hr, ps, pr, fs, fr, ys, yr):
    row, wide = lax.axis_index("row"), lax.axis_index("wide")
    core, x, upper = lax.rem(row, 2), lax.rem(row // 2, 4), row // 8
    y, z = wide // 8, lax.rem(wide, 8)

    def on_wide(t, dz):
        return lax.rem(y + t, 2) * 8 + lax.rem(z + dz + 8, 8)

    def on_row(t, dx, other=0):
        chip = lax.rem(upper + t, 2) * 4 + lax.rem(x + dx + 4, 4)
        return chip * 2 + (core if other == 0 else 1 - core)

    neighbours = [
        {"wide": on_wide(0, 1)}, {"wide": on_wide(0, -1)}, {"wide": on_wide(1, 0)},
        {"row": on_row(0, 1)}, {"row": on_row(0, -1)}, {"row": on_row(1, 0)}, {"row": on_row(0, 0, 1)},
    ]
    barrier = pltpu.get_barrier_semaphore()
    for where in neighbours:
        pl.semaphore_signal(barrier, inc=1, device_id=where, device_id_type=MESH)
    pl.semaphore_wait(barrier, len(neighbours))
    partner = {"row": on_row(0, 0, 1)}

    pivots = [(0, pv.at[0], gpv.at[0], 0, 0), (1, pv.at[1], gpv.at[1], 1, 0), (2, pv.at[2], gpv.at[2], 0, 1)]
    columns = [(3, cq, gcq, 0, None), (4, c7, gc7, 1, None), (5, wq, gwq, 0, None), (6, w7, gw7, 1, None)]
    rows = [(7, rq, grq, 0, None), (8, r7, gr7, 1, None)]
    sign = (1, -1)

    def only(job, f):
        if job[4] is None:
            f()
        else:
            pl.when(core == job[4])(f)

    def local(job):
        k, src, dst = job[:3]
        return pltpu.make_async_copy(src, dst.at[row if k >= 7 else wide], lsem.at[k])

    def across(job):
        k, src, dst = job[:3]
        if k >= 7:
            return remote(src, dst.at[row], xs.at[k], xr.at[k], {"row": on_row(1, 0)})
        return remote(src, dst.at[wide], xs.at[k], xr.at[k], {"wide": on_wide(1, 0)})

    def crossed(job):
        k, src, dst = job[:3]
        if k >= 7:
            return remote(src, dst.at[on_row(1, 0)], xs.at[k], xr.at[k], {"row": on_row(1, 0)})
        return remote(src, dst.at[on_wide(1, 0)], xs.at[k], xr.at[k], {"wide": on_wide(1, 0)})

    def hop(job, t, way, d, arriving=False):
        k, src, dst = job[:3]
        s = sign[way]
        back = d if arriving else d - 1
        if k >= 7:
            block = dst.at[on_row(t, -s * back)]
            start = src if isinstance(d, int) and d == 1 and t == 0 else block
            return remote(start, block, hs.at[k - 7, t, way, d], hr.at[k - 7, t, way, d], {"row": on_row(0, s)})
        block = dst.at[on_wide(t, -s * back)]
        start = src if isinstance(d, int) and d == 1 and t == 0 else block
        return remote(start, block, zs.at[k, t, way, d], zr.at[k, t, way, d], {"wide": on_wide(0, s)})

    def share(job, t, dx, arriving=False):
        k, src, dst = job[:3]
        block = dst.at[on_row(t, dx, 1 if arriving else 0)]
        rel = dx + 2
        return remote(block, block, fs.at[k - 7, t, rel], fr.at[k - 7, t, rel], partner)

    def sides(job):
        return (0,) if job[0] == 4 else (0, 1)

    def step_across(job, dz, arriving=False):
        block = job[2].at[on_wide(1 if arriving else 0, dz)]
        return remote(block, block, ys.at[dz + 3], yr.at[dz + 3], {"wide": on_wide(1, 0)})

    def begin(job):
        local(job).start()
        across(job).start()
        hop(job, 0, 0, 1).start()
        hop(job, 0, 1, 1).start()

    def second(job):
        if len(sides(job)) == 2:
            crossed(job).wait_recv()
            hop(job, 1, 0, 1).start()
            hop(job, 1, 1, 1).start()

    def pass_on(job, d, ways):
        for t in sides(job):
            for way in (0, 1):
                hop(job, t, way, d, True).wait_recv()
                if ways == 2 or (ways == 1 and way == job[3]):
                    hop(job, t, way, d + 1).start()
                if len(sides(job)) == 1:
                    step_across(job, -sign[way] * d).start()

    def last(job, d):
        for t in sides(job):
            hop(job, t, job[3], d, True).wait_recv()
        if len(sides(job)) == 1:
            step_across(job, -sign[job[3]] * d).start()

    for job in pivots + columns + rows:
        only(job, lambda: begin(job))
    for job in pivots + columns:
        only(job, lambda: second(job))
    for job in rows:
        local(job).wait()
        share(job, 0, 0).start()
    for job in pivots + columns:
        only(job, lambda: pass_on(job, 1, 2))
    for job in rows:
        second(job)
        share(job, 1, 0).start()
    for job in pivots + columns:
        only(job, lambda: pass_on(job, 2, 2))
    for job in rows:
        pass_on(job, 1, 1)
        for t in (0, 1):
            share(job, t, -1).start()
            share(job, t, 1).start()
    for job in pivots + columns:
        only(job, lambda: pass_on(job, 3, 1))
    for job in pivots:
        def done(job=job):
            local(job).wait()
            last(job, 4)
            remote(job[2], job[2], ps.at[job[0]], pr.at[job[0]], partner).start()
        only(job, done)
    for job in rows:
        last(job, 2)
        for t in (0, 1):
            share(job, t, -2).start()
    for job in columns:
        local(job).wait()
        last(job, 4)

    def sent(job):
        across(job).wait_send()
        full = 2 if job[0] >= 7 else 4
        if len(sides(job)) == 1:
            crossed(job).wait_recv()
            for dz in (-1, 1, -2, 2, -3, 3, 4):
                step_across(job, dz, True).wait_recv()
                step_across(job, dz).wait_send()
        for t in sides(job):
            for way in (0, 1):
                for d in range(1, full + 1 if way == job[3] else full):
                    hop(job, t, way, d).wait_send()

    for job in pivots:
        def carried(job=job):
            sent(job)
            remote(job[2], job[2], ps.at[job[0]], pr.at[job[0]], partner).wait_send()
        only(job, carried)

        @pl.when(core != job[4])
        def _():
            remote(job[2], job[2], ps.at[job[0]], pr.at[job[0]], partner).wait_recv()
    for job in columns:
        sent(job)
    for job in rows:
        sent(job)
        for t in (0, 1):
            for dx in (0, -1, 1, -2):
                share(job, t, dx, True).wait_recv()
                share(job, t, dx).wait_send()


def gather(pieces):
    outs = [piece(p.dtype, N, *p.shape) for p in PIECES[:6]] + [piece(F32, 3, N, 24, PAIR)]
    return pl.pallas_call(
        gather_kernel,
        name="gather_panels",
        out_shape=outs,
        in_specs=[ANY] * 7,
        out_specs=[VM] * 7,
        scratch_shapes=[
            pltpu.SemaphoreType.DMA((9,)),
            pltpu.SemaphoreType.DMA((9,)),
            pltpu.SemaphoreType.DMA((9,)),
            pltpu.SemaphoreType.DMA((7, 2, 2, 5)),
            pltpu.SemaphoreType.DMA((7, 2, 2, 5)),
            pltpu.SemaphoreType.DMA((2, 2, 2, 3)),
            pltpu.SemaphoreType.DMA((2, 2, 2, 3)),
            pltpu.SemaphoreType.DMA((3,)),
            pltpu.SemaphoreType.DMA((3,)),
            pltpu.SemaphoreType.DMA((2, 2, 4)),
            pltpu.SemaphoreType.DMA((2, 2, 4)),
            pltpu.SemaphoreType.DMA((8,)),
            pltpu.SemaphoreType.DMA((8,)),
        ],
        compiler_params=pltpu.CompilerParams(collective_id=0, has_side_effects=True),
    )(*pieces)


def dot(a, b):
    return jnp.dot(a, b, preferred_element_type=F32)


def split(a):
    high = a.astype(BF16)
    return high, (a - high.astype(F32)).astype(BF16)


def dot3(a, b):
    ah, al = split(a)
    bh, bl = split(b)
    return dot(ah, bh) + (dot(ah, bl) + dot(al, bh))


def invert(a_ref, out_ref, s_ref, x_ref, r_ref):
    n = PAIR
    eye = (
        lax.broadcasted_iota(jnp.int32, (n, n), 0) == lax.broadcasted_iota(jnp.int32, (n, n), 1)
    ).astype(F32)
    a = a_ref[...]
    across = lax.rsqrt(jnp.sum(a * eye, axis=0, keepdims=True))
    down = lax.rsqrt(jnp.sum(a * eye, axis=1, keepdims=True))
    s = a * across * down
    sh, sl = split(s)
    s_ref[...] = jnp.concatenate([sh, sh, sl], 1)
    bound = jnp.max(jnp.sum(jnp.abs(s), axis=1, keepdims=True), axis=0, keepdims=True)
    start = 1.9 / bound
    x_ref[...] = start * eye
    r_ref[...] = eye - start * s

    def quick(_, c):
        r = r_ref[...].astype(BF16)
        x = x_ref[...]
        both = dot(jnp.concatenate([x.astype(BF16), r], 0), r)
        x_ref[...] = x + both[:n]
        r_ref[...] = both[n:]
        return c

    lax.fori_loop(0, 5, quick, 0)

    def careful(state):
        step, _ = state
        xh, xl = split(x_ref[...])
        r = eye - dot(s_ref[...], jnp.concatenate([xh, xl, xh], 0))
        size = jnp.max(jnp.sum(jnp.abs(r), axis=1, keepdims=True))
        lost = jnp.logical_and(step == 0, jnp.logical_not(size < 0.9))
        near = size < 0.25
        r_ref[...] = r

        @pl.when(lost)
        def _():
            x_ref[...] = eye / bound

        @pl.when(jnp.logical_and(jnp.logical_not(lost), jnp.logical_not(near)))
        def _():
            x_ref[...] = x_ref[...] + dot3(x_ref[...], r_ref[...])

        @pl.when(near)
        def _():
            x = x_ref[...]
            x_ref[...] = x + dot(x.astype(BF16), r_ref[...].astype(BF16))

        return step + 1, jnp.where(lost, 1.0, size)

    lax.while_loop(lambda s: jnp.logical_and(s[0] < 64, s[1] > 1e-3), careful, (0, 1.0))
    out_ref[...] = x_ref[...] * across * down


def finish_kernel(other, pv, b0, b1, cq, c7, wq, w7, h, w, oh, ow,
                  s_ref, x_ref, r_ref, g_ref, c_ref, m_ref, b_ref, x2_ref, w_ref, h_ref, sem):
    step = pl.program_id(0)

    @pl.when(step == 0)
    def _():
        loads = [pltpu.make_async_copy(b, b_ref.at[i], sem.at[i]) for i, b in enumerate((b0, b1))]
        loads.append(pltpu.make_async_copy(h, h_ref, sem.at[2]))
        for load in loads:
            load.start()

        def keep(i, value):
            high, low = split(value)
            m_ref[i] = jnp.concatenate([high, high, low], 1)

        def times(i, value):
            high, low = split(value)
            return dot(m_ref[i], jnp.concatenate([high, low, high], 0))

        invert(pv.at[0], g_ref, s_ref, x_ref, r_ref)
        keep(0, g_ref[...])
        keep(1, pv[1].T)
        t = times(0, pv[1])
        keep(3, t)
        c_ref[...] = pv[2] - times(1, t)
        invert(c_ref, g_ref, s_ref, x_ref, r_ref)
        keep(2, g_ref[...])
        for i, panel in enumerate((wq, w7)):
            for m in range(N):
                w_ref[i, 18 * m : 18 * m + 18, :] = panel[m].astype(F32)
        for load in loads:
            load.wait()

        first = times(0, b_ref[0])
        xb = times(2, b_ref[1] - times(1, first))
        xa = first - times(3, xb)
        for i, part in enumerate((xa, xb)):
            high, low = split(part)
            x2_ref[i * PAIR : (i + 1) * PAIR, :] = high
            x2_ref[(i + 2) * PAIR : (i + 3) * PAIR, :] = low
        panels = [w_ref[i].astype(BF16) for i in (0, 1)]
        change = dot(jnp.concatenate(panels * 2, 1), x2_ref[...])
        ow[...] = (w[...].astype(F32) - change).astype(BF16)

    strip = oh.shape[0]

    def pruned(origin, shape, dim):
        place = lax.broadcasted_iota(jnp.int32, shape, dim) + origin
        begin = other[0] * PAIR
        return jnp.where(
            jnp.logical_or(
                jnp.logical_and(place >= begin, place < begin + PAIR), place >= (NPAIRS - 1) * PAIR
            ),
            1, 0,
        )

    lines = lax.axis_index("row") * 1152 + step * strip

    gone = pruned(lines, (strip, 1), 0) + pruned(lax.axis_index("wide") * 1152, (1, 1152), 1)
    change = dot(jnp.concatenate([cq[...], c7[...]], 1), x2_ref[0 : 2 * PAIR, :])
    held = h_ref[pl.ds(pl.multiple_of(step * strip, 8), strip), :]
    oh[...] = jnp.where(gone > 0, 0.0, held - change)


def finish(other, pv, b0, b1, cq, c7, wq, w7, hessian, weight):
    steps = 4
    strip = 1152 // steps

    def whole(*shape):
        return pl.BlockSpec(shape, lambda g, o: (0,) * len(shape))

    def strips(columns):
        return pl.BlockSpec((strip, columns), lambda g, o: (g, 0))

    return pl.pallas_call(
        finish_kernel,
        name="finish",
        out_shape=[piece(F32, 1152, 1152), piece(BF16, 288, 1152)],
        grid_spec=pltpu.PrefetchScalarGridSpec(
            num_scalar_prefetch=1,
            grid=(steps,),
            in_specs=[
                whole(3, PAIR, PAIR), ANY, ANY, strips(PAIR), strips(PAIR),
                whole(N, 18, PAIR), whole(N, 18, PAIR), ANY, whole(288, 1152),
            ],
            out_specs=[strips(1152), whole(288, 1152)],
            scratch_shapes=[
                pltpu.VMEM((PAIR, 3 * PAIR), BF16),
                pltpu.VMEM((PAIR, PAIR), F32),
                pltpu.VMEM((PAIR, PAIR), F32),
                pltpu.VMEM((PAIR, PAIR), F32),
                pltpu.VMEM((PAIR, PAIR), F32),
                pltpu.VMEM((4, PAIR, 3 * PAIR), BF16),
                pltpu.VMEM((2, PAIR, 1152), F32),
                pltpu.VMEM((4 * PAIR, 1152), BF16),
                pltpu.VMEM((2, 288, PAIR), F32),
                pltpu.VMEM((1152, 1152), F32),
                pltpu.SemaphoreType.DMA((3,)),
            ],
        ),
    )(other, pv, b0, b1, cq, c7, wq, w7, hessian, weight)


def cut_kernel(block, hc, hr, hp, h7, wc, w7, ocq, owq, opq, orq, oc7, ow7):
    for m in range(N // 2):
        ocq[m] = hc[72 * m : 72 * m + 72, :].astype(BF16)
        oc7[m] = h7[72 * m : 72 * m + 72, :].astype(BF16)
        orq[m] = hr[24 * m : 24 * m + 24, :]
        opq[m] = hp[24 * m : 24 * m + 24, :]
    for src, out in ((wc, owq), (w7, ow7)):
        full = src[...].astype(F32)
        for m in range(N // 2):
            out[m] = full[18 * m : 18 * m + 18, :].astype(BF16)


def cut(block, hessian, weight):
    half = N // 2

    def out(*shape):
        return pl.BlockSpec((half, *shape), lambda g, b: (g, 0, 0))

    return pl.pallas_call(
        cut_kernel,
        name="cut",
        out_shape=[
            piece(BF16, N, 72, PAIR), piece(BF16, N, 18, PAIR), piece(F32, N, 24, PAIR),
            piece(F32, N, 24, 1152), piece(BF16, N, 72, PAIR), piece(BF16, N, 18, PAIR),
        ],
        grid_spec=pltpu.PrefetchScalarGridSpec(
            num_scalar_prefetch=1,
            grid=(2,),
            in_specs=[
                pl.BlockSpec((576, PAIR), lambda g, b: (g, b[0])),
                pl.BlockSpec((192, 1152), lambda g, b: (2 * b[0] + g, 0)),
                pl.BlockSpec((192, PAIR), lambda g, b: (2 * b[0] + g, b[0])),
                pl.BlockSpec((576, PAIR), lambda g, b: (g, 2)),
                pl.BlockSpec((144, PAIR), lambda g, b: (g, b[0])),
                pl.BlockSpec((144, PAIR), lambda g, b: (g, 2)),
            ],
            out_specs=[out(72, PAIR), out(18, PAIR), out(24, PAIR), out(24, 1152), out(72, PAIR), out(18, PAIR)],
        ),
    )(block, hessian, hessian, hessian, hessian, weight, weight)


def per_device(hessian, weight, pairs):
    tile = hessian.shape[0]
    per_tile = tile // PAIR
    other = jnp.minimum(pairs[0], pairs[1])
    root = other // per_tile
    block = (other % per_tile).reshape(1)
    cq, wq, pq, rq, c7, w7 = cut(block, hessian, weight)
    operands = (cq, wq, pq, rq, c7, w7, hessian)
    pieces = lax.switch(root, [functools.partial(scatter, i) for i in range(N)], *operands)
    gcq, gwq, grq, gc7, gw7, gr7, gpv = gather(pieces)

    return finish(
        other.reshape(1), gpv.reshape(3, PAIR, PAIR), grq.reshape(PAIR, tile), gr7.reshape(PAIR, tile),
        gcq.reshape(tile, PAIR), gc7.reshape(tile, PAIR), gwq, gw7, hessian, weight,
    )


def solution(mesh):
    return jax.shard_map(
        per_device,
        mesh=mesh,
        in_specs=(P("row", "wide"), P("row", "wide"), P()),
        out_specs=(P("row", "wide"), P("row", "wide")),
        check_vma=False,
    )
```

```python
import functools

import jax
import jax.numpy as jnp
from jax import lax
from jax.experimental import pallas as pl
from jax.experimental.pallas import tpu as pltpu
from jax.sharding import PartitionSpec as P

HEAD = 192
PAIR = 2 * HEAD
NPAIRS = 48
N = 16
LAST = N - 1
MESH = pl.DeviceIdType.MESH
F32 = jnp.float32
BF16 = jnp.bfloat16
ANY = pl.BlockSpec(memory_space=pl.ANY)
VM = pl.BlockSpec(memory_space=pltpu.VMEM)


def remote(src, dst, send, recv, where):
    return pltpu.make_async_remote_copy(
        src_ref=src, dst_ref=dst, send_sem=send, recv_sem=recv,
        device_id=where, device_id_type=MESH,
    )


def greet_holders(root):
    row, wide = lax.axis_index("row"), lax.axis_index("wide")
    barrier = pltpu.get_barrier_semaphore()
    peers = 0
    for axis, me in (("wide", wide), ("row", row)):
        for holder in sorted({root, LAST}):
            @pl.when(me != holder)
            def _():
                pl.semaphore_signal(barrier, inc=1, device_id={axis: holder}, device_id_type=MESH)

            peers = peers + jnp.where(me == holder, N - 1, 0)

    @pl.when(peers > 0)
    def _():
        pl.semaphore_wait(barrier, peers)


def scatter_kernel(root, cq, wq, pq, rq, c7, w7, r7,
                   ocq, owq, orq, oc7, ow7, or7, opv, pst, ssem, rsem, lsem):
    row, wide = lax.axis_index("row"), lax.axis_index("wide")
    greet_holders(root)
    at_wide, at_row = wide == root, row == root
    last_wide, last_row = wide == LAST, row == LAST

    def strip(m, columns):
        return r7.at[pl.ds(pl.multiple_of(2 * PAIR + 24 * m, 8), 24), columns]

    jobs = [
        (0, jnp.logical_and(at_row, at_wide), at_row, "wide", wide, lambda m: pq.at[m], pst.at[0]),
        (1, jnp.logical_and(at_row, last_wide), at_row, "wide", wide, lambda m: rq.at[m, :, pl.ds(2 * PAIR, PAIR)], pst.at[1]),
        (2, jnp.logical_and(last_row, last_wide), last_row, "wide", wide, lambda m: strip(m, pl.ds(2 * PAIR, PAIR)), pst.at[2]),
        (3, at_row, None, "row", row, lambda m: rq.at[m], orq),
        (4, last_row, None, "row", row, lambda m: strip(m, slice(None)), or7),
        (5, at_wide, None, "wide", wide, lambda m: cq.at[m], ocq),
        (6, last_wide, None, "wide", wide, lambda m: c7.at[m], oc7),
        (7, at_wide, None, "wide", wide, lambda m: wq.at[m], owq),
        (8, last_wide, None, "wide", wide, lambda m: w7.at[m], ow7),
    ]

    def spread(job, act):
        k, mine, _, axis, me, src, dst = job

        @pl.when(mine)
        def _():
            def body(m, _):
                @pl.when(m != me)
                def _():
                    copy = remote(src(m), dst, ssem.at[k, m], rsem.at[k], {axis: m})
                    copy.start() if act == "start" else copy.wait_send()

                @pl.when(m == me)
                def _():
                    copy = pltpu.make_async_copy(src(m), dst, lsem.at[k])
                    copy.start() if act == "start" else copy.wait()
                return 0

            lax.fori_loop(0, N, body, 0)

    def arrive(job):
        k, mine, group, axis, me, src, dst = job
        away = jnp.logical_not(mine)
        if group is not None:
            away = jnp.logical_and(away, group)

        @pl.when(away)
        def _():
            remote(src(0), dst, ssem.at[k, 0], rsem.at[k], {axis: 0}).wait_recv()

    for job in jobs:
        spread(job, "start")
    for job in jobs[:3]:
        arrive(job)
        spread(job, "drain")
    second = [(9, at_row, 0, 0, root), (10, at_row, 1, 0, root), (11, last_row, 2, 1, LAST)]

    def forward(item, act):
        k, mine, part, core, origin = item

        @pl.when(mine)
        def _():
            def body(h, _):
                m = 2 * h + core

                @pl.when(m != origin)
                def _():
                    copy = remote(pst.at[part], opv.at[part], ssem.at[k, m], rsem.at[k], {"row": m})
                    copy.start() if act == "start" else copy.wait_send()

                @pl.when(m == origin)
                def _():
                    copy = pltpu.make_async_copy(pst.at[part], opv.at[part], lsem.at[k])
                    copy.start() if act == "start" else copy.wait()
                return 0

            lax.fori_loop(0, N // 2, body, 0)

    for item in second:
        forward(item, "start")
    for item in second:
        k, mine, part, core, origin = item
        away = jnp.logical_and(jnp.logical_not(mine), lax.rem(row, 2) == core)

        @pl.when(away)
        def _():
            remote(pst.at[part], opv.at[part], ssem.at[k, 0], rsem.at[k], {"row": 0}).wait_recv()

    for job in jobs[3:]:
        arrive(job)
    for item in second:
        forward(item, "drain")
    for job in jobs[3:]:
        spread(job, "drain")


def piece(dtype, *shape):
    return jax.ShapeDtypeStruct(shape, dtype)


PIECES = [
    piece(BF16, 72, PAIR), piece(BF16, 18, PAIR), piece(F32, 24, 1152),
    piece(BF16, 72, PAIR), piece(BF16, 18, PAIR), piece(F32, 24, 1152),
    piece(F32, 3, 24, PAIR),
]


def scatter(root, *operands):
    outs = PIECES + [piece(F32, 3, 24, PAIR)]
    return pl.pallas_call(
        functools.partial(scatter_kernel, root),
        name=f"scatter_{root}",
        out_shape=outs,
        in_specs=[ANY] * 7,
        out_specs=[ANY] * 8,
        scratch_shapes=[
            pltpu.SemaphoreType.DMA((12, N)),
            pltpu.SemaphoreType.DMA((12,)),
            pltpu.SemaphoreType.DMA((12,)),
        ],
        compiler_params=pltpu.CompilerParams(collective_id=1 + root, has_side_effects=True),
    )(*operands)[:7]


def gather_kernel(cq, wq, rq, c7, w7, r7, pv,
                  gcq, gwq, grq, gc7, gw7, gr7, gpv,
                  lsem, xs, xr, zs, zr, hs, hr, ps, pr, fs, fr, ys, yr):
    row, wide = lax.axis_index("row"), lax.axis_index("wide")
    core, x, upper = lax.rem(row, 2), lax.rem(row // 2, 4), row // 8
    y, z = wide // 8, lax.rem(wide, 8)

    def on_wide(t, dz):
        return lax.rem(y + t, 2) * 8 + lax.rem(z + dz + 8, 8)

    def on_row(t, dx, other=0):
        chip = lax.rem(upper + t, 2) * 4 + lax.rem(x + dx + 4, 4)
        return chip * 2 + (core if other == 0 else 1 - core)

    neighbours = [
        {"wide": on_wide(0, 1)}, {"wide": on_wide(0, -1)}, {"wide": on_wide(1, 0)},
        {"row": on_row(0, 1)}, {"row": on_row(0, -1)}, {"row": on_row(1, 0)}, {"row": on_row(0, 0, 1)},
    ]
    barrier = pltpu.get_barrier_semaphore()
    for where in neighbours:
        pl.semaphore_signal(barrier, inc=1, device_id=where, device_id_type=MESH)
    pl.semaphore_wait(barrier, len(neighbours))
    partner = {"row": on_row(0, 0, 1)}

    pivots = [(0, pv.at[0], gpv.at[0], 0, 0), (1, pv.at[1], gpv.at[1], 1, 0), (2, pv.at[2], gpv.at[2], 0, 1)]
    columns = [(3, cq, gcq, 0, None), (4, c7, gc7, 1, None), (5, wq, gwq, 0, None), (6, w7, gw7, 1, None)]
    rows = [(7, rq, grq, 0, None), (8, r7, gr7, 1, None)]
    sign = (1, -1)

    def only(job, f):
        if job[4] is None:
            f()
        else:
            pl.when(core == job[4])(f)

    def local(job):
        k, src, dst = job[:3]
        return pltpu.make_async_copy(src, dst.at[row if k >= 7 else wide], lsem.at[k])

    def across(job):
        k, src, dst = job[:3]
        if k >= 7:
            return remote(src, dst.at[row], xs.at[k], xr.at[k], {"row": on_row(1, 0)})
        return remote(src, dst.at[wide], xs.at[k], xr.at[k], {"wide": on_wide(1, 0)})

    def crossed(job):
        k, src, dst = job[:3]
        if k >= 7:
            return remote(src, dst.at[on_row(1, 0)], xs.at[k], xr.at[k], {"row": on_row(1, 0)})
        return remote(src, dst.at[on_wide(1, 0)], xs.at[k], xr.at[k], {"wide": on_wide(1, 0)})

    def hop(job, t, way, d, arriving=False):
        k, src, dst = job[:3]
        s = sign[way]
        back = d if arriving else d - 1
        if k >= 7:
            block = dst.at[on_row(t, -s * back)]
            start = src if isinstance(d, int) and d == 1 and t == 0 else block
            return remote(start, block, hs.at[k - 7, t, way, d], hr.at[k - 7, t, way, d], {"row": on_row(0, s)})
        block = dst.at[on_wide(t, -s * back)]
        start = src if isinstance(d, int) and d == 1 and t == 0 else block
        return remote(start, block, zs.at[k, t, way, d], zr.at[k, t, way, d], {"wide": on_wide(0, s)})

    def share(job, t, dx, arriving=False):
        k, src, dst = job[:3]
        block = dst.at[on_row(t, dx, 1 if arriving else 0)]
        rel = dx + 2
        return remote(block, block, fs.at[k - 7, t, rel], fr.at[k - 7, t, rel], partner)

    def sides(job):
        return (0,) if job[0] == 4 else (0, 1)

    def step_across(job, dz, arriving=False):
        block = job[2].at[on_wide(1 if arriving else 0, dz)]
        return remote(block, block, ys.at[dz + 3], yr.at[dz + 3], {"wide": on_wide(1, 0)})

    def begin(job):
        local(job).start()
        across(job).start()
        hop(job, 0, 0, 1).start()
        hop(job, 0, 1, 1).start()

    def second(job):
        if len(sides(job)) == 2:
            crossed(job).wait_recv()
            hop(job, 1, 0, 1).start()
            hop(job, 1, 1, 1).start()

    def pass_on(job, d, ways):
        for t in sides(job):
            for way in (0, 1):
                hop(job, t, way, d, True).wait_recv()
                if ways == 2 or (ways == 1 and way == job[3]):
                    hop(job, t, way, d + 1).start()
                if len(sides(job)) == 1:
                    step_across(job, -sign[way] * d).start()

    def last(job, d):
        for t in sides(job):
            hop(job, t, job[3], d, True).wait_recv()
        if len(sides(job)) == 1:
            step_across(job, -sign[job[3]] * d).start()

    for job in pivots + columns + rows:
        only(job, lambda: begin(job))
    for job in pivots + columns:
        only(job, lambda: second(job))
    for job in rows:
        local(job).wait()
        share(job, 0, 0).start()
    for job in pivots + columns:
        only(job, lambda: pass_on(job, 1, 2))
    for job in rows:
        second(job)
        share(job, 1, 0).start()
    for job in pivots + columns:
        only(job, lambda: pass_on(job, 2, 2))
    for job in rows:
        pass_on(job, 1, 1)
        for t in (0, 1):
            share(job, t, -1).start()
            share(job, t, 1).start()
    for job in pivots + columns:
        only(job, lambda: pass_on(job, 3, 1))
    for job in pivots:
        def done(job=job):
            local(job).wait()
            last(job, 4)
            remote(job[2], job[2], ps.at[job[0]], pr.at[job[0]], partner).start()
        only(job, done)
    for job in rows:
        last(job, 2)
        for t in (0, 1):
            share(job, t, -2).start()
    for job in columns:
        local(job).wait()
        last(job, 4)

    def sent(job):
        across(job).wait_send()
        full = 2 if job[0] >= 7 else 4
        if len(sides(job)) == 1:
            crossed(job).wait_recv()
            for dz in (-1, 1, -2, 2, -3, 3, 4):
                step_across(job, dz, True).wait_recv()
                step_across(job, dz).wait_send()
        for t in sides(job):
            for way in (0, 1):
                for d in range(1, full + 1 if way == job[3] else full):
                    hop(job, t, way, d).wait_send()

    for job in pivots:
        def carried(job=job):
            sent(job)
            remote(job[2], job[2], ps.at[job[0]], pr.at[job[0]], partner).wait_send()
        only(job, carried)

        @pl.when(core != job[4])
        def _():
            remote(job[2], job[2], ps.at[job[0]], pr.at[job[0]], partner).wait_recv()
    for job in columns:
        sent(job)
    for job in rows:
        sent(job)
        for t in (0, 1):
            for dx in (0, -1, 1, -2):
                share(job, t, dx, True).wait_recv()
                share(job, t, dx).wait_send()


def gather(pieces):
    outs = [piece(p.dtype, N, *p.shape) for p in PIECES[:6]] + [piece(F32, 3, N, 24, PAIR)]
    return pl.pallas_call(
        gather_kernel,
        name="gather_panels",
        out_shape=outs,
        in_specs=[ANY] * 7,
        out_specs=[VM] * 7,
        scratch_shapes=[
            pltpu.SemaphoreType.DMA((9,)),
            pltpu.SemaphoreType.DMA((9,)),
            pltpu.SemaphoreType.DMA((9,)),
            pltpu.SemaphoreType.DMA((7, 2, 2, 5)),
            pltpu.SemaphoreType.DMA((7, 2, 2, 5)),
            pltpu.SemaphoreType.DMA((2, 2, 2, 3)),
            pltpu.SemaphoreType.DMA((2, 2, 2, 3)),
            pltpu.SemaphoreType.DMA((3,)),
            pltpu.SemaphoreType.DMA((3,)),
            pltpu.SemaphoreType.DMA((2, 2, 4)),
            pltpu.SemaphoreType.DMA((2, 2, 4)),
            pltpu.SemaphoreType.DMA((8,)),
            pltpu.SemaphoreType.DMA((8,)),
        ],
        compiler_params=pltpu.CompilerParams(collective_id=0, has_side_effects=True),
    )(*pieces)


def dot(a, b):
    return jnp.dot(a, b, preferred_element_type=F32)


def split(a):
    high = a.astype(BF16)
    return high, (a - high.astype(F32)).astype(BF16)


def dot3(a, b):
    ah, al = split(a)
    bh, bl = split(b)
    return dot(ah, bh) + (dot(ah, bl) + dot(al, bh))


def invert(a_ref, out_ref, s_ref, x_ref, r_ref):
    n = PAIR
    eye = (
        lax.broadcasted_iota(jnp.int32, (n, n), 0) == lax.broadcasted_iota(jnp.int32, (n, n), 1)
    ).astype(F32)
    a = a_ref[...]
    across = lax.rsqrt(jnp.sum(a * eye, axis=0, keepdims=True))
    down = lax.rsqrt(jnp.sum(a * eye, axis=1, keepdims=True))
    s = a * across * down
    sh, sl = split(s)
    s_ref[...] = jnp.concatenate([sh, sh, sl], 1)
    bound = jnp.max(jnp.sum(jnp.abs(s), axis=1, keepdims=True), axis=0, keepdims=True)
    start = 1.9 / bound
    x_ref[...] = start * eye
    r_ref[...] = eye - start * s

    def quick(_, c):
        r = r_ref[...].astype(BF16)
        x = x_ref[...]
        both = dot(jnp.concatenate([x.astype(BF16), r], 0), r)
        x_ref[...] = x + both[:n]
        r_ref[...] = both[n:]
        return c

    lax.fori_loop(0, 5, quick, 0)

    def careful(state):
        step, _ = state
        xh, xl = split(x_ref[...])
        r = eye - dot(s_ref[...], jnp.concatenate([xh, xl, xh], 0))
        size = jnp.max(jnp.sum(jnp.abs(r), axis=1, keepdims=True))
        lost = jnp.logical_and(step == 0, jnp.logical_not(size < 0.9))
        near = size < 0.25
        r_ref[...] = r

        @pl.when(lost)
        def _():
            x_ref[...] = eye / bound

        @pl.when(jnp.logical_and(jnp.logical_not(lost), jnp.logical_not(near)))
        def _():
            x_ref[...] = x_ref[...] + dot3(x_ref[...], r_ref[...])

        @pl.when(near)
        def _():
            x = x_ref[...]
            x_ref[...] = x + dot(x.astype(BF16), r_ref[...].astype(BF16))

        return step + 1, jnp.where(lost, 1.0, size)

    lax.while_loop(lambda s: jnp.logical_and(s[0] < 64, s[1] > 1e-3), careful, (0, 1.0))
    out_ref[...] = x_ref[...] * across * down


def finish_kernel(other, pv, b0, b1, cq, c7, wq, w7, h, w, oh, ow,
                  s_ref, x_ref, r_ref, g_ref, c_ref, m_ref, b_ref, x2_ref, w_ref, h_ref, sem):
    step = pl.program_id(0)

    @pl.when(step == 0)
    def _():
        loads = [pltpu.make_async_copy(b, b_ref.at[i], sem.at[i]) for i, b in enumerate((b0, b1))]
        loads.append(pltpu.make_async_copy(h, h_ref, sem.at[2]))
        for load in loads:
            load.start()

        def keep(i, value):
            high, low = split(value)
            m_ref[i] = jnp.concatenate([high, high, low], 1)

        def times(i, value):
            high, low = split(value)
            return dot(m_ref[i], jnp.concatenate([high, low, high], 0))

        invert(pv.at[0], g_ref, s_ref, x_ref, r_ref)
        keep(0, g_ref[...])
        keep(1, pv[1].T)
        t = times(0, pv[1])
        keep(3, t)
        c_ref[...] = pv[2] - times(1, t)
        invert(c_ref, g_ref, s_ref, x_ref, r_ref)
        keep(2, g_ref[...])
        for i, panel in enumerate((wq, w7)):
            for m in range(N):
                w_ref[i, 18 * m : 18 * m + 18, :] = panel[m].astype(F32)
        for load in loads:
            load.wait()

        first = times(0, b_ref[0])
        xb = times(2, b_ref[1] - times(1, first))
        xa = first - times(3, xb)
        for i, part in enumerate((xa, xb)):
            high, low = split(part)
            x2_ref[i * PAIR : (i + 1) * PAIR, :] = high
            x2_ref[(i + 2) * PAIR : (i + 3) * PAIR, :] = low
        panels = [w_ref[i].astype(BF16) for i in (0, 1)]
        change = dot(jnp.concatenate(panels * 2, 1), x2_ref[...])
        ow[...] = (w[...].astype(F32) - change).astype(BF16)

    strip = oh.shape[0]

    def pruned(origin, shape, dim):
        place = lax.broadcasted_iota(jnp.int32, shape, dim) + origin
        begin = other[0] * PAIR
        return jnp.where(
            jnp.logical_or(
                jnp.logical_and(place >= begin, place < begin + PAIR), place >= (NPAIRS - 1) * PAIR
            ),
            1, 0,
        )

    lines = lax.axis_index("row") * 1152 + step * strip

    gone = pruned(lines, (strip, 1), 0) + pruned(lax.axis_index("wide") * 1152, (1, 1152), 1)
    change = dot(jnp.concatenate([cq[...], c7[...]], 1), x2_ref[0 : 2 * PAIR, :])
    held = h_ref[pl.ds(pl.multiple_of(step * strip, 8), strip), :]
    oh[...] = jnp.where(gone > 0, 0.0, held - change)


def finish(other, pv, b0, b1, cq, c7, wq, w7, hessian, weight):
    steps = 4
    strip = 1152 // steps

    def whole(*shape):
        return pl.BlockSpec(shape, lambda g, o: (0,) * len(shape))

    def strips(columns):
        return pl.BlockSpec((strip, columns), lambda g, o: (g, 0))

    return pl.pallas_call(
        finish_kernel,
        name="finish",
        out_shape=[piece(F32, 1152, 1152), piece(BF16, 288, 1152)],
        grid_spec=pltpu.PrefetchScalarGridSpec(
            num_scalar_prefetch=1,
            grid=(steps,),
            in_specs=[
                whole(3, PAIR, PAIR), ANY, ANY, strips(PAIR), strips(PAIR),
                whole(N, 18, PAIR), whole(N, 18, PAIR), ANY, whole(288, 1152),
            ],
            out_specs=[strips(1152), whole(288, 1152)],
            scratch_shapes=[
                pltpu.VMEM((PAIR, 3 * PAIR), BF16),
                pltpu.VMEM((PAIR, PAIR), F32),
                pltpu.VMEM((PAIR, PAIR), F32),
                pltpu.VMEM((PAIR, PAIR), F32),
                pltpu.VMEM((PAIR, PAIR), F32),
                pltpu.VMEM((4, PAIR, 3 * PAIR), BF16),
                pltpu.VMEM((2, PAIR, 1152), F32),
                pltpu.VMEM((4 * PAIR, 1152), BF16),
                pltpu.VMEM((2, 288, PAIR), F32),
                pltpu.VMEM((1152, 1152), F32),
                pltpu.SemaphoreType.DMA((3,)),
            ],
        ),
    )(other, pv, b0, b1, cq, c7, wq, w7, hessian, weight)


def cut_kernel(block, hc, hr, hp, h7, wc, w7, ocq, owq, opq, orq, oc7, ow7):
    for m in range(N // 2):
        ocq[m] = hc[72 * m : 72 * m + 72, :].astype(BF16)
        oc7[m] = h7[72 * m : 72 * m + 72, :].astype(BF16)
        orq[m] = hr[24 * m : 24 * m + 24, :]
        opq[m] = hp[24 * m : 24 * m + 24, :]
    for src, out in ((wc, owq), (w7, ow7)):
        full = src[...].astype(F32)
        for m in range(N // 2):
            out[m] = full[18 * m : 18 * m + 18, :].astype(BF16)


def cut(block, hessian, weight):
    half = N // 2

    def out(*shape):
        return pl.BlockSpec((half, *shape), lambda g, b: (g, 0, 0))

    return pl.pallas_call(
        cut_kernel,
        name="cut",
        out_shape=[
            piece(BF16, N, 72, PAIR), piece(BF16, N, 18, PAIR), piece(F32, N, 24, PAIR),
            piece(F32, N, 24, 1152), piece(BF16, N, 72, PAIR), piece(BF16, N, 18, PAIR),
        ],
        grid_spec=pltpu.PrefetchScalarGridSpec(
            num_scalar_prefetch=1,
            grid=(2,),
            in_specs=[
                pl.BlockSpec((576, PAIR), lambda g, b: (g, b[0])),
                pl.BlockSpec((192, 1152), lambda g, b: (2 * b[0] + g, 0)),
                pl.BlockSpec((192, PAIR), lambda g, b: (2 * b[0] + g, b[0])),
                pl.BlockSpec((576, PAIR), lambda g, b: (g, 2)),
                pl.BlockSpec((144, PAIR), lambda g, b: (g, b[0])),
                pl.BlockSpec((144, PAIR), lambda g, b: (g, 2)),
            ],
            out_specs=[out(72, PAIR), out(18, PAIR), out(24, PAIR), out(24, 1152), out(72, PAIR), out(18, PAIR)],
        ),
    )(block, hessian, hessian, hessian, hessian, weight, weight)


def per_device(hessian, weight, pairs):
    tile = hessian.shape[0]
    per_tile = tile // PAIR
    other = jnp.minimum(pairs[0], pairs[1])
    root = other // per_tile
    block = (other % per_tile).reshape(1)
    cq, wq, pq, rq, c7, w7 = cut(block, hessian, weight)
    operands = (cq, wq, pq, rq, c7, w7, hessian)
    pieces = lax.switch(root, [functools.partial(scatter, i) for i in range(N)], *operands)
    gcq, gwq, grq, gc7, gw7, gr7, gpv = gather(pieces)

    return finish(
        other.reshape(1), gpv.reshape(3, PAIR, PAIR), grq.reshape(PAIR, tile), gr7.reshape(PAIR, tile),
        gcq.reshape(tile, PAIR), gc7.reshape(tile, PAIR), gwq, gw7, hessian, weight,
    )


def solution(mesh):
    return jax.shard_map(
        per_device,
        mesh=mesh,
        in_specs=(P("row", "wide"), P("row", "wide"), P()),
        out_specs=(P("row", "wide"), P("row", "wide")),
        check_vma=False,
    )
```
